256 devices in a mesh: tm: 64 (over y, z, core), region: 4 (over x).
Axes of the slice: x: 4, y: 4, z: 8, core: 2. Of those that a mesh axis runs over, the one named last changes fastest.
Arguments:
- covariates: bfloat16 [8, 8192, 256], P('region', 'tm'), may hold values from -4 to 4
- observed: float32 [8, 8192, 256], P('region', 'tm'), may hold values from -40 to 40
- input_weight: bfloat16 [256, 256], replicated, may hold values from -0.375 to 0.375
- filter_weight: bfloat16 [3, 512, 512], replicated, may hold values from -0.25 to 0.25
- mixing_weight: bfloat16 [3, 256, 256], replicated, may hold values from -0.375 to 0.375
- output_weight: bfloat16 [256, 4096], replicated, may hold values from -0.375 to 0.375
Outputs:
- covariate_grad: bfloat16 [8, 8192, 256], P('region', 'tm')
- input_grad: bfloat16 [256, 256], P('tm')
- filter_grad: bfloat16 [3, 512, 512], P(None, 'tm')
- mixing_grad: bfloat16 [3, 256, 256], P(None, 'tm')
- output_grad: bfloat16 [256, 4096], P('tm')
The draws below stay inside these ranges and needn't reach their ends.
All inputs are finite; a program needn't handle non-finite values.
Results may differ from the reference program's by a relative error of at most 0.022.
Values may be sent and summed in bfloat16 or wider, within the bound.
No kernel may reach another device: no remote copies, remote signals or barrier semaphores. Data moves between devices by JAX's collectives and lax.ppermute only.
A program may use at most 64 MiB of HBM per device.

```python
import math
import jax
import jax.numpy as jnp
from jax import lax

NODES = 256
WIDTH = 256
SCENARIOS = 16
LAYERS = 3
SEQS = 8
STEPS = 8192


def draw_observed(key, part):
    key_base, key_nodes = jax.random.split(key, 2)
    position = jnp.arange(STEPS, dtype=jnp.float32) / (STEPS - 1)
    ramp = 0.05 * jnp.exp(math.log(60.0) * position)
    node_scale = jnp.exp(jax.random.uniform(key_nodes, (SEQS, 1, NODES), jnp.float32, math.log(0.3), math.log(3.0)))
    base = jnp.clip(jax.random.normal(key_base, (SEQS, STEPS, NODES), jnp.float32), -4.0, 4.0)
    return (base * ramp[None, :, None] * node_scale).astype(jnp.float32)


def draw_output_weight(key, part):
    key_entries, key_order, key_jitter = jax.random.split(jax.random.fold_in(key, 7), 3)
    order = jax.random.permutation(key_order, SCENARIOS).astype(jnp.float32)
    jitter = jax.random.uniform(key_jitter, (SCENARIOS,), jnp.float32, 0.0, 1.0)
    factor = jnp.exp(math.log(0.1) * (order + jitter) / SCENARIOS)
    column_factor = jnp.repeat(factor, NODES)
    entries = jax.random.normal(key_entries, (WIDTH, SCENARIOS * NODES), jnp.float32)
    values = entries * WIDTH ** (-0.5) * column_factor[None, :]
    return jnp.clip(values, -0.375, 0.375).astype(jnp.bfloat16)


def levels(stream_key, dims, pieces, least, largest):
    def one(axis_at, shards_of):
        draws = jax.random.uniform(jax.random.fold_in(jax.random.fold_in(stream_key, 6), axis_at), (shards_of,), jnp.float32, least / len(pieces), largest / len(pieces))
        return jnp.repeat(jnp.exp(draws), dims[axis_at] // shards_of).reshape((-1,) + (1,) * (len(dims) - axis_at - 1))

    factor_of = one(*pieces[0])
    for cut in pieces[1:]:
        factor_of = factor_of * one(*cut)
    return factor_of


def gaussian(own_key, dims, deviation, limit, cuts=(), held_as=jnp.bfloat16):
    loudness = levels(own_key, dims, cuts, -0.22, 0.18) if cuts else 1.0
    result = jax.random.normal(own_key, dims, jnp.float32) * deviation * loudness
    return jnp.minimum(jnp.maximum(result, -limit), limit).astype(held_as)


def setup_inputs(seed: int = 0) -> dict:
    streams_of = jax.random.split(jax.random.key(seed), 7)
    covariates = gaussian(streams_of[0], (SEQS, STEPS, NODES), 1.0, 4.0, ((0, 4), (1, 64)))
    observed = draw_observed(jax.random.fold_in(streams_of[6], 71), 0)
    input_weight = gaussian(streams_of[2], (NODES, WIDTH), NODES ** -0.5, 0.375)
    filter_weight = gaussian(streams_of[3], (LAYERS, 2 * WIDTH, 2 * WIDTH), (2 * WIDTH) ** -0.5, 0.25)
    mixing_weight = gaussian(streams_of[4], (LAYERS, WIDTH, WIDTH), WIDTH ** -0.5, 0.375)
    output_weight = draw_output_weight(jax.random.fold_in(streams_of[6], 71), 0)
    return {"covariates": covariates, "observed": observed, "input_weight": input_weight, "filter_weight": filter_weight, "mixing_weight": mixing_weight, "output_weight": output_weight}


epsilon = 1e-05

def energy(predicted, observed, scenarios):
    node_count = observed.shape[-1]
    scenario_vals = predicted.reshape(predicted.shape[:-1] + (scenarios, node_count))
    gram_matrix = jnp.einsum('...sn,...rn->...sr', scenario_vals, scenario_vals, precision=lax.Precision.HIGHEST)
    against = jnp.einsum('...sn,...n->...s', scenario_vals, observed, precision=lax.Precision.HIGHEST)
    own_sq = jnp.diagonal(gram_matrix, axis1=-2, axis2=-1)
    target = lax.optimization_barrier(jnp.sum(observed * observed, axis=-1))
    to_target = jnp.sqrt((own_sq - 2.0 * against + target[..., None]) / node_count + epsilon)
    off_diag = 1.0 - jnp.eye(scenarios, dtype=jnp.float32)
    pair_sq = (own_sq[..., :, None] + own_sq[..., None, :] - 2.0 * gram_matrix) / node_count
    between = jnp.sqrt(pair_sq * off_diag + epsilon) * off_diag
    return lax.optimization_barrier(jnp.mean(to_target, axis=-1)) - lax.optimization_barrier(jnp.sum(between, axis=(-2, -1))) / (2.0 * scenarios * (scenarios - 1))

def network(weights, cov_seq):
    w_input, w_filter, w_mixing, w_output = weights
    length = cov_seq.shape[0]
    hidden = jnp.dot(cov_seq, w_input, preferred_element_type=jnp.float32).astype(jnp.bfloat16)
    channels = hidden.shape[-1]
    for layer_no in range(w_filter.shape[0]):
        dilation = 2 ** layer_no
        delayed = jnp.pad(hidden, ((dilation, 0), (0, 0)))[:length]
        joined = jnp.concatenate([delayed, hidden], axis=-1)
        preact = jnp.dot(joined, w_filter[layer_no], preferred_element_type=jnp.float32)
        gated = (jnp.tanh(preact[:, :channels]) * jax.nn.sigmoid(preact[:, channels:])).astype(jnp.bfloat16)
        hidden = (hidden.astype(jnp.float32) + jnp.dot(gated, w_mixing[layer_no], preferred_element_type=jnp.float32)).astype(jnp.bfloat16)
    return jnp.dot(hidden, w_output, preferred_element_type=jnp.float32)

def reference(covariates, observed, input_weight, filter_weight, mixing_weight, output_weight):
    scale = jnp.sqrt(lax.optimization_barrier(jnp.mean(observed * observed, axis=(1, 2))) + epsilon)
    weights = (input_weight.astype(jnp.float32), filter_weight.astype(jnp.float32), mixing_weight.astype(jnp.float32), output_weight.astype(jnp.float32))

    def per_sequence(running, inputs_seq):
        cov_seq, obs_seq, seq_scale = inputs_seq

        def scoring(weight_set, cov_part):
            return jnp.sum(energy(network(weight_set, cov_part), obs_seq, SCENARIOS)) / seq_scale
        _, pull_back = jax.vjp(scoring, weights, cov_seq)
        grads_w, grad_cov = pull_back(jnp.ones((), jnp.float32))
        running = tuple((first + second for first, second in zip(running, grads_w)))
        return (running, grad_cov)
    zeros_init = tuple((jnp.zeros_like(weight_one) for weight_one in weights))
    totals, covariate_grad = lax.scan(per_sequence, zeros_init, (covariates, observed, scale))
    return (covariate_grad, totals[0].astype(jnp.bfloat16), totals[1].astype(jnp.bfloat16), totals[2].astype(jnp.bfloat16), totals[3].astype(jnp.bfloat16))
```

```python
import functools

import jax
import jax.numpy as jnp
from jax import lax
from jax.experimental import pallas as pl
from jax.experimental.pallas import tpu as pltpu
from jax.sharding import Mesh
from jax.sharding import PartitionSpec as P

epsilon = 1e-05

NODES = 256
SCENARIOS = 16
LAYERS = 3
HALO = 8
ROWS = 128
BLOCK = ROWS + 2 * HALO
SEQ = 2
ALL_ROWS = SEQ * BLOCK
HEAD = ROWS + HALO
ALL_HEAD = SEQ * HEAD
TM = ("y", "z", "core")
F32 = jnp.float32
BF16 = jnp.bfloat16
VMEM = pltpu.VMEM
PARAMS = pltpu.CompilerParams(vmem_limit_bytes=48 * 1024 * 1024)


def mm(a, b):
    return jnp.dot(a, b, preferred_element_type=F32)


def mm_nt(a, b):
    return lax.dot_general(a, b, (((1,), (1,)), ((), ())), preferred_element_type=F32)


def vmem_specs(count):
    return [pl.BlockSpec(memory_space=VMEM)] * count


def shape(dims, dtype):
    return jax.ShapeDtypeStruct(dims, dtype)


def start_kernel(cov, obs, to_next, to_prev, squares):
    for b in range(SEQ):
        to_next[b] = cov[b, ROWS - HALO :, :]
        to_prev[b, :, :NODES] = cov[b, :HALO, :].astype(F32)
        to_prev[b, :, NODES:] = obs[b, :HALO, :]
        sq = obs[b] * obs[b]
        by_lane = jnp.sum(sq, axis=0, keepdims=True)
        total = jnp.sum(by_lane, axis=1, keepdims=True)
        squares[:, b, :] = jnp.broadcast_to(total, (squares.shape[0], 128))


def own_rows(x):
    return jnp.concatenate([x[HALO : HALO + ROWS], x[BLOCK + HALO : BLOCK + HALO + ROWS]], axis=0)


def permutation(core, group):
    i = lax.broadcasted_iota(jnp.int32, (NODES, NODES), 0)
    c = lax.broadcasted_iota(jnp.int32, (NODES, NODES), 1)
    half = i // 128
    inner = i % 128
    side = jnp.where(half == 0, 1 - core, core)
    wanted = (inner // group) * (2 * group) + side * group + inner % group
    return jnp.where(c == wanted, 1.0, 0.0).astype(BF16)


def energy_rows(y, o):
    inv_nodes = 1.0 / NODES

    def distance(a, b):
        d0 = a[0] - b[0]
        d1 = a[1] - b[1]
        return jnp.sum(d0 * d0 + d1 * d1, axis=1, keepdims=True)

    alpha = [
        lax.rsqrt(distance(y[s], o) * inv_nodes + epsilon) * (1.0 / (SCENARIOS * NODES))
        for s in range(SCENARIOS)
    ]
    factor = 1.0 / (SCENARIOS * (SCENARIOS - 1) * NODES)
    beta = {}
    for s in range(SCENARIOS):
        for r in range(s + 1, SCENARIOS):
            beta[s, r] = lax.rsqrt(distance(y[s], y[r]) * inv_nodes + epsilon) * factor
    result = []
    for s in range(SCENARIOS):
        gamma = alpha[s]
        acc = [-(alpha[s] * o[0]), -(alpha[s] * o[1])]
        for r in range(SCENARIOS):
            if r == s:
                continue
            weight = beta[min(s, r), max(s, r)]
            gamma = gamma - weight
            acc = [acc[0] + weight * y[r][0], acc[1] + weight * y[r][1]]
        result.append(jnp.concatenate([acc[0] + gamma * y[s][0], acc[1] + gamma * y[s][1]], axis=1))
    return result


def forward_kernel(
    place, from_prev, cov, from_next, obs, w_in, w_f, w_m, w_out,
    tanh_out, gate_out, dpred, cov_t, gated_t, last_t, taps_t,
    pred, target,
):
    core = place[0]
    perm4 = permutation(core, 4)
    perm8 = permutation(core, 8)

    def turned(perm, x):
        return mm_nt(perm, own_rows(x).astype(BF16)).astype(BF16)

    pieces = []
    for b in range(SEQ):
        pieces += [
            from_prev[b].astype(F32),
            cov[b].astype(F32),
            from_next[b, :, :NODES],
        ]
    x = jnp.concatenate(pieces, axis=0)
    cov_t[...] = turned(perm4, x)
    hidden = mm(x.astype(BF16), w_in[...]).astype(BF16)
    for layer in range(LAYERS):
        wide = hidden.astype(F32)
        delayed_wide = pltpu.roll(wide, 2**layer, 0)
        delayed = delayed_wide.astype(BF16)
        taps_t[layer, 0] = turned(perm8, delayed_wide)
        taps_t[layer, 1] = turned(perm8, wide)
        preact = mm(delayed, w_f[layer, :NODES, :]) + mm(hidden, w_f[layer, NODES:, :])
        filter_act = jnp.tanh(preact[:, :NODES])
        gate_act = jax.nn.sigmoid(preact[:, NODES:])
        tanh_out[layer] = filter_act
        gate_out[layer] = gate_act
        gated = (filter_act * gate_act).astype(BF16)
        gated_t[layer] = turned(perm4, gated.astype(F32))
        hidden = (wide + mm(gated, w_m[layer])).astype(BF16)
    wide = hidden.astype(F32)
    last_t[...] = turned(perm4, wide)
    head = jnp.concatenate([wide[HALO:BLOCK], wide[BLOCK + HALO :]], axis=0).astype(BF16)
    pred[...] = mm(head, w_out[...])
    for b in range(SEQ):
        target[b * HEAD : b * HEAD + ROWS, :] = obs[b]
        target[b * HEAD + ROWS : (b + 1) * HEAD, :] = from_next[b, :, NODES:]

    def step(i, carry):
        halves = []
        for part in range(2):
            at = pl.ds(pl.multiple_of(i * 16 + part * 8, 8), 8)
            y = [
                (pred[at, s * NODES : s * NODES + 128], pred[at, s * NODES + 128 : (s + 1) * NODES])
                for s in range(SCENARIOS)
            ]
            o = (target[at, :128], target[at, 128:])
            halves.append(energy_rows(y, o))
        at = pl.ds(pl.multiple_of(i * 16, 16), 16)
        for s in range(SCENARIOS):
            both = jnp.concatenate([halves[0][s], halves[1][s]], axis=0)
            dpred[at, s * NODES : (s + 1) * NODES] = both.astype(BF16)
        return carry

    lax.fori_loop(0, ALL_HEAD // 16, step, 0)


def backward_kernel(
    place, sums, tanh_in, gate_in, dpred, cov_t, gated_t, last_t, taps_t, w_in, w_f, w_m, w_out,
    cov_grad, send, keep,
):
    at_end = place[1]
    steps = ROWS * place[2]
    total = jnp.sum(sums[...], axis=0)
    inv = lax.rsqrt(total / (steps * NODES).astype(F32) + epsilon)
    inv = jnp.concatenate([inv, inv], axis=1)
    places = ((send, 0), (keep, 1))

    head_grad = mm_nt(dpred[...], w_out[...])
    pieces = []
    for b in range(SEQ):
        scaled = head_grad[b * HEAD : (b + 1) * HEAD] * inv[b : b + 1, :]
        row = lax.broadcasted_iota(jnp.int32, (HEAD, NODES), 0)
        scaled = jnp.where((row >= ROWS) & (at_end == 1), 0.0, scaled)
        pieces += [jnp.zeros((HALO, NODES), F32), scaled]
    grad = jnp.concatenate(pieces, axis=0).astype(BF16)

    for x in range(4):
        columns = slice(x * 1024, (x + 1) * 1024)
        out_grad = None
        for b in range(SEQ):
            part = mm(
                last_t[:, b * ROWS : (b + 1) * ROWS],
                dpred[b * HEAD : b * HEAD + ROWS, columns],
            ) * inv[b : b + 1, :1]
            out_grad = part if out_grad is None else out_grad + part
        for ref, half in places:
            for y in range(4):
                top = half * 128 + y * 32
                ref[x, y, :, :1024] = out_grad[top : top + 32].astype(BF16)

    def store_small(x, value):
        for ref, half in places:
            for y in range(4):
                top = half * 128 + y * 32
                ref[x, y, :, 1024:1280] = value[top : top + 32].astype(BF16)

    for layer in reversed(range(LAYERS)):
        grad_wide = grad.astype(F32)
        store_small(layer, mm(gated_t[layer], own_rows(grad_wide).astype(BF16)))
        gated_cot = mm_nt(grad, w_m[layer]).astype(BF16).astype(F32)
        filter_act = tanh_in[layer]
        gate_act = gate_in[layer]
        grad_preact = jnp.concatenate(
            [
                gated_cot * gate_act * (1.0 - filter_act * filter_act),
                gated_cot * filter_act * gate_act * (1.0 - gate_act),
            ],
            axis=1,
        )
        own_preact = own_rows(grad_preact).astype(BF16)
        grad_preact = grad_preact.astype(BF16)
        for tap in range(2):
            tap_grad = mm(taps_t[layer, tap], own_preact)
            for ref, half in places:
                for y_low in range(2):
                    top = half * 128 + y_low * 64
                    for x in range(4):
                        columns = slice(x * 128, (x + 1) * 128)
                        for low in range(2):
                            base = 1280 + low * 384 + layer * 128
                            ref[x, tap * 2 + y_low, :, base : base + 128] = tap_grad[
                                top + low * 32 : top + low * 32 + 32, columns
                            ].astype(BF16)
        grad_joined = mm_nt(grad_preact, w_f[layer]).astype(BF16)
        past = grad_joined[:, :NODES].astype(F32)
        now = grad_joined[:, NODES:].astype(F32)
        earlier = pltpu.roll(past, ALL_ROWS - 2**layer, 0)
        grad = ((grad_wide + now).astype(BF16).astype(F32) + earlier).astype(BF16)
    own = own_rows(grad.astype(F32)).astype(BF16)
    store_small(3, mm(cov_t[...], own))
    result = mm_nt(own, w_in[...]).astype(BF16)
    for b in range(SEQ):
        cov_grad[b] = result[b * ROWS : (b + 1) * ROWS]


def add_kernel(a, b, out):
    out[...] = (a[...].astype(F32) + b[...].astype(F32)).astype(BF16)


def plane_kernel(pieces, out):
    total = pieces[0].astype(F32)
    for i in range(1, pieces.shape[0]):
        total = total + pieces[i].astype(F32)
    for z in range(8):
        r = slice(z * 4, z * 4 + 4)
        first = jnp.concatenate([total[r, :512], total[r, 1024:1152]], axis=1)
        second = jnp.concatenate([total[r, 512:1024], total[r, 1152:1280]], axis=1)
        low = z % 4
        base = 1280 + (z // 4) * 384
        taps = total[low * 8 : low * 8 + 8, base : base + 384]
        both = jnp.concatenate([first, second], axis=0)
        out[z] = jnp.concatenate([both, taps], axis=1).astype(BF16)


def line_kernel(pieces, out):
    total = pieces[0].astype(F32)
    for i in range(1, pieces.shape[0]):
        total = total + pieces[i].astype(F32)
    out[...] = total.astype(BF16)


def finish_kernel(g, input_grad, filter_grad, mixing_grad, output_grad):
    for x in range(4):
        v = g[x].astype(F32)
        output_grad[:, x * 1024 : x * 1024 + 512] = v[:4, :512].astype(BF16)
        output_grad[:, x * 1024 + 512 : (x + 1) * 1024] = v[4:, :512].astype(BF16)
        small = jnp.concatenate([v[:4, 512:640], v[4:, 512:640]], axis=1).astype(BF16)
        if x < LAYERS:
            mixing_grad[x] = small
        else:
            input_grad[...] = small
        for layer in range(LAYERS):
            base = 640 + layer * 128
            filter_grad[layer, :, x * 128 : (x + 1) * 128] = v[:, base : base + 128].astype(BF16)


def call(kernel, out_shape, count, scratch=(), scalars=False):
    specs = vmem_specs(count)
    if scalars:
        specs = [pl.BlockSpec(memory_space=pltpu.SMEM)] + specs
    outs = jax.tree.map(lambda _: pl.BlockSpec(memory_space=VMEM), out_shape)
    return pl.pallas_call(
        kernel,
        out_shape=out_shape,
        in_specs=specs,
        out_specs=outs,
        scratch_shapes=scratch,
        compiler_params=PARAMS,
    )


def per_device(cov, obs, w_in, w_f, w_m, w_out):
    count = lax.axis_size(TM)
    me = lax.axis_index(TM)
    place = jnp.stack(
        [
            lax.axis_index("core"),
            jnp.where(me == count - 1, 1, 0),
            jnp.int32(count),
        ]
    ).astype(jnp.int32)
    to_next, to_prev, squares = call(
        start_kernel,
        (
            shape((SEQ, HALO, NODES), BF16),
            shape((SEQ, HALO, 2 * NODES), F32),
            shape((count, SEQ, 128), F32),
        ),
        2,
    )(cov, obs)
    from_prev = lax.ppermute(to_next, TM, [(i, i + 1) for i in range(count - 1)])
    from_next = lax.ppermute(to_prev, TM, [(i + 1, i) for i in range(count - 1)])
    sums = lax.all_to_all(squares, TM, 0, 0, tiled=True)

    saved = call(
        forward_kernel,
        (
            shape((LAYERS, ALL_ROWS, NODES), F32),
            shape((LAYERS, ALL_ROWS, NODES), F32),
            shape((ALL_HEAD, SCENARIOS * NODES), BF16),
            shape((NODES, SEQ * ROWS), BF16),
            shape((LAYERS, NODES, SEQ * ROWS), BF16),
            shape((NODES, SEQ * ROWS), BF16),
            shape((LAYERS, 2, NODES, SEQ * ROWS), BF16),
        ),
        8,
        scratch=[
            pltpu.VMEM((ALL_HEAD, SCENARIOS * NODES), F32),
            pltpu.VMEM((ALL_HEAD, NODES), F32),
        ],
        scalars=True,
    )(place, from_prev, cov, from_next, obs, w_in, w_f, w_m, w_out)

    piece = shape((4, 4, 32, 2048), BF16)
    cov_grad, send, keep = call(
        backward_kernel,
        (shape((SEQ, ROWS, NODES), BF16), piece, piece),
        12,
        scalars=True,
    )(place, sums, *saved, w_in, w_f, w_m, w_out)

    got = lax.ppermute(send, "core", [(0, 1), (1, 0)])
    chip = call(add_kernel, piece, 2)(keep, got)
    plane = lax.all_to_all(chip.reshape(16, 32, 2048), ("x", "y"), 0, 0, tiled=True)
    by_z = call(plane_kernel, shape((8, 8, 1024), BF16), 1)(plane)
    line = lax.all_to_all(by_z, "z", 0, 0, tiled=True)
    mine = call(line_kernel, shape((8, 1024), BF16), 1)(line)
    whole = lax.all_gather(mine, "x")
    input_grad, filter_grad, mixing_grad, output_grad = call(
        finish_kernel,
        (
            shape((4, NODES), BF16),
            shape((LAYERS, 8, 2 * NODES), BF16),
            shape((LAYERS, 4, NODES), BF16),
            shape((4, SCENARIOS * NODES), BF16),
        ),
        1,
    )(whole)
    return (cov_grad, input_grad, filter_grad, mixing_grad, output_grad)


def solution(mesh):
    inner = Mesh(mesh.devices.reshape(4, 8, 2, 4), ("y", "z", "core", "x"))
    data = P("x", TM, None)
    return jax.shard_map(
        per_device,
        mesh=inner,
        in_specs=(data, data, P(), P(), P(), P()),
        out_specs=(data, P(TM, None), P(None, TM, None), P(None, TM, None), P(TM, None)),
        check_vma=False,
    )
```

```python
import jax
import jax.numpy as jnp
from jax import lax
from jax.experimental import pallas as pl
from jax.experimental.pallas import tpu as pltpu
from jax.sharding import Mesh
from jax.sharding import PartitionSpec as P

epsilon = 1e-05

NODES = 256
SCENARIOS = 16
LAYERS = 3
HALO = 8
ROWS = 128
BLOCK = ROWS + 2 * HALO
SEQ = 2
ALL_ROWS = SEQ * BLOCK
HEAD = ROWS + HALO
ALL_HEAD = SEQ * HEAD
TM = ("y", "z", "core")
F32 = jnp.float32
BF16 = jnp.bfloat16
VMEM = pltpu.VMEM


def mm(a, b):
    return jnp.dot(a, b, preferred_element_type=F32)


def mm_nt(a, b):
    return lax.dot_general(a, b, (((1,), (1,)), ((), ())), preferred_element_type=F32)


def shape(dims, dtype):
    return jax.ShapeDtypeStruct(dims, dtype)


def edge_kernel(cov_tail, cov_head, obs_head, to_next, to_prev):
    for b in range(SEQ):
        to_next[b] = cov_tail[b].astype(F32)[HALO:].astype(BF16)
        to_prev[b, :, :NODES] = cov_head[b].astype(F32)[:HALO]
        to_prev[b, :, NODES:] = obs_head[b]


def square_kernel(obs, before, after, squares):
    for b in range(SEQ):
        sq = obs[b] * obs[b]
        by_lane = jnp.sum(sq, axis=0, keepdims=True)
        total = jnp.sum(by_lane, axis=1, keepdims=True)
        squares[:, b, :] = jnp.broadcast_to(total, (squares.shape[0], 128))


def own_rows(x):
    return jnp.concatenate([x[HALO : HALO + ROWS], x[BLOCK + HALO : BLOCK + HALO + ROWS]], axis=0)


def permutation(core, group):
    i = lax.broadcasted_iota(jnp.int32, (NODES, NODES), 0)
    c = lax.broadcasted_iota(jnp.int32, (NODES, NODES), 1)
    half = i // 128
    inner = i % 128
    side = jnp.where(half == 0, 1 - core, core)
    wanted = (inner // group) * (2 * group) + side * group + inner % group
    return jnp.where(c == wanted, 1.0, 0.0).astype(BF16)


def energy_rows(y, o):
    inv_nodes = 1.0 / NODES

    def distance(a, b):
        d0 = a[0] - b[0]
        d1 = a[1] - b[1]
        return jnp.sum(d0 * d0 + d1 * d1, axis=1, keepdims=True)

    alpha = [
        lax.rsqrt(distance(y[s], o) * inv_nodes + epsilon) * (1.0 / (SCENARIOS * NODES))
        for s in range(SCENARIOS)
    ]
    factor = 1.0 / (SCENARIOS * (SCENARIOS - 1) * NODES)
    beta = {}
    for s in range(SCENARIOS):
        for r in range(s + 1, SCENARIOS):
            beta[s, r] = lax.rsqrt(distance(y[s], y[r]) * inv_nodes + epsilon) * factor
    result = []
    for s in range(SCENARIOS):
        gamma = alpha[s]
        acc = [-(alpha[s] * o[0]), -(alpha[s] * o[1])]
        for r in range(SCENARIOS):
            if r == s:
                continue
            weight = beta[min(s, r), max(s, r)]
            gamma = gamma - weight
            acc = [acc[0] + weight * y[r][0], acc[1] + weight * y[r][1]]
        result.append(jnp.concatenate([acc[0] + gamma * y[s][0], acc[1] + gamma * y[s][1]], axis=1))
    return result


def forward_kernel(
    place, from_prev, from_next, cov_hbm, obs_hbm, w_in_hbm, w_f_hbm, w_m_hbm, w_out_hbm,
    tanh_hbm, gate_hbm, dpred_hbm, cov_t_hbm, gated_t_hbm, last_t_hbm, taps_t_hbm,
    pred, target, cov, obs, w_in, w_f, w_m, w_out,
    tanh_out, gate_out, dpred, cov_t, gated_t, last_t, taps_t, sems, out_sems,
):
    cov_copy = pltpu.make_async_copy(cov_hbm, cov, sems.at[0])
    w_in_copy = pltpu.make_async_copy(w_in_hbm, w_in, sems.at[1])
    w_f_copy = pltpu.make_async_copy(w_f_hbm, w_f, sems.at[2])
    w_m_copy = pltpu.make_async_copy(w_m_hbm, w_m, sems.at[3])
    obs_copy = pltpu.make_async_copy(obs_hbm, obs, sems.at[4])
    w_out_copy = pltpu.make_async_copy(w_out_hbm, w_out, sems.at[5])
    for copy in (cov_copy, w_in_copy, w_f_copy, w_m_copy, obs_copy, w_out_copy):
        copy.start()
    core = place[0]
    perm4 = permutation(core, 4)
    perm8 = permutation(core, 8)

    def turned(perm, x):
        return mm_nt(perm, own_rows(x).astype(BF16)).astype(BF16)

    cov_copy.wait()
    pieces = []
    for b in range(SEQ):
        pieces += [
            from_prev[b].astype(F32),
            cov[b].astype(F32),
            from_next[b, :, :NODES],
        ]
    x = jnp.concatenate(pieces, axis=0)
    cov_t[...] = turned(perm4, x)
    w_in_copy.wait()
    hidden = mm(x.astype(BF16), w_in[...]).astype(BF16)
    w_f_copy.wait()
    w_m_copy.wait()
    for layer in range(LAYERS):
        wide = hidden.astype(F32)
        delayed_wide = pltpu.roll(wide, 2**layer, 0)
        delayed = delayed_wide.astype(BF16)
        taps_t[layer, 0] = turned(perm8, delayed_wide)
        taps_t[layer, 1] = turned(perm8, wide)
        preact = mm(delayed, w_f[layer, :NODES, :]) + mm(hidden, w_f[layer, NODES:, :])
        filter_act = jnp.tanh(preact[:, :NODES])
        gate_act = jax.nn.sigmoid(preact[:, NODES:])
        tanh_out[layer] = filter_act
        gate_out[layer] = gate_act
        gated = (filter_act * gate_act).astype(BF16)
        gated_t[layer] = turned(perm4, gated.astype(F32))
        hidden = (wide + mm(gated, w_m[layer])).astype(BF16)
    wide = hidden.astype(F32)
    last_t[...] = turned(perm4, wide)
    head = jnp.concatenate([wide[HALO:BLOCK], wide[BLOCK + HALO :]], axis=0).astype(BF16)
    w_out_copy.wait()
    pred[...] = mm(head, w_out[...])
    obs_copy.wait()
    for b in range(SEQ):
        target[b * HEAD : b * HEAD + ROWS, :] = obs[b]
        target[b * HEAD + ROWS : (b + 1) * HEAD, :] = from_next[b, :, NODES:]

    stores = [
        pltpu.make_async_copy(tanh_out, tanh_hbm, out_sems.at[0]),
        pltpu.make_async_copy(gate_out, gate_hbm, out_sems.at[1]),
        pltpu.make_async_copy(cov_t, cov_t_hbm, out_sems.at[2]),
        pltpu.make_async_copy(gated_t, gated_t_hbm, out_sems.at[3]),
        pltpu.make_async_copy(last_t, last_t_hbm, out_sems.at[4]),
        pltpu.make_async_copy(taps_t, taps_t_hbm, out_sems.at[5]),
    ]
    for copy in stores:
        copy.start()

    def step(i, carry):
        halves = []
        for part in range(2):
            at = pl.ds(pl.multiple_of(i * 16 + part * 8, 8), 8)
            y = [
                (pred[at, s * NODES : s * NODES + 128], pred[at, s * NODES + 128 : (s + 1) * NODES])
                for s in range(SCENARIOS)
            ]
            o = (target[at, :128], target[at, 128:])
            halves.append(energy_rows(y, o))
        at = pl.ds(pl.multiple_of(i * 16, 16), 16)
        for s in range(SCENARIOS):
            both = jnp.concatenate([halves[0][s], halves[1][s]], axis=0)
            dpred[at, s * NODES : (s + 1) * NODES] = both.astype(BF16)
        return carry

    first, last = 0, 0
    for part, last in enumerate((12, ALL_HEAD // 16)):
        lax.fori_loop(first, last, step, 0)
        rows = pl.ds(first * 16, (last - first) * 16)
        copy = pltpu.make_async_copy(dpred.at[rows], dpred_hbm.at[rows], out_sems.at[6 + part])
        copy.start()
        stores.append(copy)
        first = last
    for copy in stores:
        copy.wait()


def backward_kernel(
    place, sums, tanh_hbm, gate_hbm, dpred_hbm, cov_t_hbm, gated_t_hbm, last_t_hbm, taps_t_hbm,
    w_in_hbm, w_f_hbm, w_m_hbm, w_out_hbm,
    cov_grad, send, keep,
    tanh_in, gate_in, dpred, cov_t, gated_t, last_t, taps_t, w_in, w_f, w_m, w_out, sems,
):
    copies = [pltpu.make_async_copy(last_t_hbm, last_t, sems.at[0])]
    for x in range(4):
        columns = pl.ds(x * 1024, 1024)
        copies.append(
            pltpu.make_async_copy(dpred_hbm.at[:, columns], dpred.at[:, columns], sems.at[1 + x])
        )
    copies.append(pltpu.make_async_copy(w_out_hbm, w_out, sems.at[5]))
    later = (
        (w_m_hbm, w_m),
        (gated_t_hbm, gated_t),
        (tanh_hbm, tanh_in),
        (gate_hbm, gate_in),
        (w_f_hbm, w_f),
        (taps_t_hbm, taps_t),
        (cov_t_hbm, cov_t),
        (w_in_hbm, w_in),
    )
    for k, (source, target) in enumerate(later):
        copies.append(pltpu.make_async_copy(source, target, sems.at[6 + k]))
    for copy in copies:
        copy.start()
    copies[0].wait()
    at_end = place[1]
    steps = ROWS * place[2]
    total = jnp.sum(sums[...], axis=0)
    inv = lax.rsqrt(total / (steps * NODES).astype(F32) + epsilon)
    inv = jnp.concatenate([inv, inv], axis=1)
    for x in range(4):
        columns = slice(x * 1024, (x + 1) * 1024)
        out_grad = None
        copies[1 + x].wait()
        for b in range(SEQ):
            part = mm(
                last_t[:, b * ROWS : (b + 1) * ROWS],
                dpred[b * HEAD : b * HEAD + ROWS, columns],
            ) * inv[b : b + 1, :1]
            out_grad = part if out_grad is None else out_grad + part
        for ref, half in ((send, 0), (keep, 1)):
            for y in range(4):
                top = half * 128 + y * 32
                ref[x, y, :, :1024] = out_grad[top : top + 32].astype(BF16)
    copies[5].wait()
    head_grad = mm_nt(dpred[...], w_out[...])
    pieces = []
    for b in range(SEQ):
        scaled = head_grad[b * HEAD : (b + 1) * HEAD] * inv[b : b + 1, :]
        row = lax.broadcasted_iota(jnp.int32, (HEAD, NODES), 0)
        scaled = jnp.where((row >= ROWS) & (at_end == 1), 0.0, scaled)
        pieces += [jnp.zeros((HALO, NODES), F32), scaled]
    grad = jnp.concatenate(pieces, axis=0).astype(BF16)
    for copy in copies[6:]:
        copy.wait()
    places = ((send, 0), (keep, 1))

    def store_small(x, value):
        for ref, half in places:
            for y in range(4):
                top = half * 128 + y * 32
                ref[x, y, :, 1024:1280] = value[top : top + 32].astype(BF16)

    for layer in reversed(range(LAYERS)):
        grad_wide = grad.astype(F32)
        store_small(layer, mm(gated_t[layer], own_rows(grad_wide).astype(BF16)))
        gated_cot = mm_nt(grad, w_m[layer]).astype(BF16).astype(F32)
        filter_act = tanh_in[layer]
        gate_act = gate_in[layer]
        grad_preact = jnp.concatenate(
            [
                gated_cot * gate_act * (1.0 - filter_act * filter_act),
                gated_cot * filter_act * gate_act * (1.0 - gate_act),
            ],
            axis=1,
        )
        own_preact = own_rows(grad_preact).astype(BF16)
        grad_preact = grad_preact.astype(BF16)
        for tap in range(2):
            tap_grad = mm(taps_t[layer, tap], own_preact)
            for ref, half in places:
                for y_low in range(2):
                    top = half * 128 + y_low * 64
                    for x in range(4):
                        columns = slice(x * 128, (x + 1) * 128)
                        for low in range(2):
                            base = 1280 + low * 384 + layer * 128
                            ref[x, tap * 2 + y_low, :, base : base + 128] = tap_grad[
                                top + low * 32 : top + low * 32 + 32, columns
                            ].astype(BF16)
        grad_joined = mm_nt(grad_preact, w_f[layer]).astype(BF16)
        past = grad_joined[:, :NODES].astype(F32)
        now = grad_joined[:, NODES:].astype(F32)
        earlier = pltpu.roll(past, ALL_ROWS - 2**layer, 0)
        grad = ((grad_wide + now).astype(BF16).astype(F32) + earlier).astype(BF16)
    own = own_rows(grad.astype(F32)).astype(BF16)
    store_small(3, mm(cov_t[...], own))
    result = mm_nt(own, w_in[...]).astype(BF16)
    for b in range(SEQ):
        cov_grad[b] = result[b * ROWS : (b + 1) * ROWS]


def add_kernel(keep, got, out):
    out[...] = keep[...] + got[...]


def plane_kernel(pieces, out):
    total = pieces[0].astype(F32)
    for i in range(1, pieces.shape[0]):
        total = total + pieces[i].astype(F32)
    for z in range(8):
        r = slice(z * 4, z * 4 + 4)
        first = jnp.concatenate([total[r, :512], total[r, 1024:1152]], axis=1)
        second = jnp.concatenate([total[r, 512:1024], total[r, 1152:1280]], axis=1)
        low = z % 4
        base = 1280 + (z // 4) * 384
        taps = total[low * 8 : low * 8 + 8, base : base + 384]
        both = jnp.concatenate([first, second], axis=0)
        out[z] = jnp.concatenate([both, taps], axis=1).astype(BF16)


def line_kernel(pieces, out):
    total = pieces[0].astype(F32)
    for i in range(1, pieces.shape[0]):
        total = total + pieces[i].astype(F32)
    out[...] = total.astype(BF16)


def finish_kernel(g, input_grad, filter_grad, mixing_grad, output_grad):
    for x in range(4):
        v = g[x].astype(F32)
        output_grad[:, x * 1024 : x * 1024 + 512] = v[:4, :512].astype(BF16)
        output_grad[:, x * 1024 + 512 : (x + 1) * 1024] = v[4:, :512].astype(BF16)
        small = jnp.concatenate([v[:4, 512:640], v[4:, 512:640]], axis=1).astype(BF16)
        if x < LAYERS:
            mixing_grad[x] = small
        else:
            input_grad[...] = small
        for layer in range(LAYERS):
            base = 640 + layer * 128
            filter_grad[layer, :, x * 128 : (x + 1) * 128] = v[:, base : base + 128].astype(BF16)


BACKWARD_LIMIT = 58
HBM = pl.BlockSpec(memory_space=pltpu.HBM)
ANY = pl.BlockSpec(memory_space=pl.ANY)
SCALARS = pl.BlockSpec(memory_space=pltpu.SMEM)
WHOLE = pl.BlockSpec(memory_space=VMEM)


def call(kernel, out_shape, in_specs, scratch=(), limit=16, name=None, out_spec=WHOLE):
    return pl.pallas_call(
        kernel,
        out_shape=out_shape,
        in_specs=in_specs,
        out_specs=jax.tree.map(lambda _: out_spec, out_shape),
        scratch_shapes=scratch,
        compiler_params=pltpu.CompilerParams(vmem_limit_bytes=limit * 1024 * 1024),
        name=name,
    )


def per_device(cov, obs, w_in, w_f, w_m, w_out):
    count = lax.axis_size(TM)
    me = lax.axis_index(TM)
    place = jnp.stack(
        [
            lax.axis_index("core"),
            jnp.where(me == count - 1, 1, 0),
            jnp.int32(count),
        ]
    ).astype(jnp.int32)
    to_next, to_prev = pl.pallas_call(
        edge_kernel,
        grid=(1,),
        in_specs=[
            pl.BlockSpec((SEQ, 16, NODES), lambda i: (0, ROWS // 16 - 1, 0)),
            pl.BlockSpec((SEQ, 16, NODES), lambda i: (0, 0, 0)),
            pl.BlockSpec((SEQ, HALO, NODES), lambda i: (0, 0, 0)),
        ],
        out_specs=(WHOLE, WHOLE),
        out_shape=(shape((SEQ, HALO, NODES), BF16), shape((SEQ, HALO, 2 * NODES), F32)),
        name="edges",
    )(cov, cov, obs)
    from_prev = lax.ppermute(to_next, TM, [(i, i + 1) for i in range(count - 1)])
    from_next = lax.ppermute(to_prev, TM, [(i + 1, i) for i in range(count - 1)])
    squares = pl.pallas_call(
        square_kernel,
        grid=(1,),
        in_specs=[pl.BlockSpec((SEQ, ROWS, NODES), lambda i: (0, 0, 0)), ANY, ANY],
        out_specs=WHOLE,
        out_shape=shape((count, SEQ, 128), F32),
        name="squares",
    )(obs, from_prev, from_next)
    sums = lax.all_to_all(squares, TM, 0, 0, tiled=True)

    saved_shapes = (
        shape((LAYERS, ALL_ROWS, NODES), F32),
        shape((LAYERS, ALL_ROWS, NODES), F32),
        shape((ALL_HEAD, SCENARIOS * NODES), BF16),
        shape((NODES, SEQ * ROWS), BF16),
        shape((LAYERS, NODES, SEQ * ROWS), BF16),
        shape((NODES, SEQ * ROWS), BF16),
        shape((LAYERS, 2, NODES, SEQ * ROWS), BF16),
    )
    saved = call(
        forward_kernel,
        saved_shapes,
        [SCALARS, WHOLE, WHOLE] + [HBM] * 6,
        scratch=[
            VMEM((ALL_HEAD, SCENARIOS * NODES), F32),
            VMEM((ALL_HEAD, NODES), F32),
            VMEM(cov.shape, BF16),
            VMEM(obs.shape, F32),
            VMEM(w_in.shape, BF16),
            VMEM(w_f.shape, BF16),
            VMEM(w_m.shape, BF16),
            VMEM(w_out.shape, BF16),
            *(VMEM(saved.shape, saved.dtype) for saved in saved_shapes),
            pltpu.SemaphoreType.DMA((6,)),
            pltpu.SemaphoreType.DMA((8,)),
        ],
        limit=60,
        name="forward",
        out_spec=HBM,
    )(place, from_prev, from_next, cov, obs, w_in, w_f, w_m, w_out)

    piece = shape((4, 4, 32, 2048), BF16)
    cov_grad, send, keep = call(
        backward_kernel,
        (shape((SEQ, ROWS, NODES), BF16), piece, piece),
        [SCALARS, WHOLE] + [HBM] * 11,
        scratch=[
            *(VMEM(saved.shape, saved.dtype) for saved in saved_shapes),
            *(VMEM(w.shape, BF16) for w in (w_in, w_f, w_m, w_out)),
            pltpu.SemaphoreType.DMA((14,)),
        ],
        limit=BACKWARD_LIMIT,
        name="backward",
    )(place, sums, *saved, w_in, w_f, w_m, w_out)
    got = lax.ppermute(send, "core", [(0, 1), (1, 0)])
    chip = call(add_kernel, piece, [WHOLE] * 2, limit=4, name="pair")(keep, got)
    plane = lax.all_to_all(chip.reshape(16, 32, 2048), ("x", "y"), 0, 0, tiled=True)
    by_z = call(plane_kernel, shape((8, 8, 1024), BF16), [WHOLE], limit=4, name="plane")(plane)
    line = lax.all_to_all(by_z, "z", 0, 0, tiled=True)
    mine = call(line_kernel, shape((8, 1024), BF16), [WHOLE], limit=4, name="line")(line)
    whole = lax.all_gather(mine, "x")
    input_grad, filter_grad, mixing_grad, output_grad = call(
        finish_kernel,
        (
            shape((4, NODES), BF16),
            shape((LAYERS, 8, 2 * NODES), BF16),
            shape((LAYERS, 4, NODES), BF16),
            shape((4, SCENARIOS * NODES), BF16),
        ),
        [WHOLE],
        limit=4,
        name="finish",
    )(whole)
    return (cov_grad, input_grad, filter_grad, mixing_grad, output_grad)


def solution(mesh):
    inner = Mesh(mesh.devices.reshape(4, 8, 2, 4), ("y", "z", "core", "x"))
    data = P("x", TM, None)
    return jax.shard_map(
        per_device,
        mesh=inner,
        in_specs=(data, data, P(), P(), P(), P()),
        out_specs=(data, P(TM, None), P(None, TM, None), P(None, TM, None), P(TM, None)),
        check_vma=False,
    )
```

```python
import jax
import jax.numpy as jnp
from jax import lax
from jax.experimental import pallas as pl
from jax.experimental.pallas import tpu as pltpu
from jax.sharding import Mesh
from jax.sharding import PartitionSpec as P

epsilon = 1e-05

NODES = 256
SCENARIOS = 16
LAYERS = 3
HALO = 8
ROWS = 128
BLOCK = ROWS + 2 * HALO
SEQ = 2
ALL_ROWS = SEQ * BLOCK
HEAD = ROWS + HALO
ALL_HEAD = SEQ * HEAD
TM = ("y", "z", "core")
F32 = jnp.float32
BF16 = jnp.bfloat16
VMEM = pltpu.VMEM


def mm(a, b):
    return jnp.dot(a, b, preferred_element_type=F32)


def mm_nt(a, b):
    return lax.dot_general(a, b, (((1,), (1,)), ((), ())), preferred_element_type=F32)


def shape(dims, dtype):
    return jax.ShapeDtypeStruct(dims, dtype)


def start_kernel(cov_hbm, obs_hbm, to_next, to_prev, squares, tail, head, obs, sems):
    copies = [
        pltpu.make_async_copy(obs_hbm, obs, sems.at[0]),
        pltpu.make_async_copy(cov_hbm.at[:, pl.ds(ROWS - 16, 16), :], tail, sems.at[1]),
        pltpu.make_async_copy(cov_hbm.at[:, pl.ds(0, 16), :], head, sems.at[2]),
    ]
    for copy in copies:
        copy.start()
    for copy in copies:
        copy.wait()
    for b in range(SEQ):
        to_next[b] = tail[b].astype(F32)[16 - HALO :].astype(BF16)
        to_prev[b, :, :NODES] = head[b].astype(F32)[:HALO]
        to_prev[b, :, NODES:] = obs[b, :HALO, :]
        sq = obs[b] * obs[b]
        by_lane = jnp.sum(sq, axis=0, keepdims=True)
        total = jnp.sum(by_lane, axis=1, keepdims=True)
        squares[:, b, :] = jnp.broadcast_to(total, (squares.shape[0], 128))


def own_rows(x):
    return jnp.concatenate([x[HALO : HALO + ROWS], x[BLOCK + HALO : BLOCK + HALO + ROWS]], axis=0)


def permutation(core, group):
    i = lax.broadcasted_iota(jnp.int32, (NODES, NODES), 0)
    c = lax.broadcasted_iota(jnp.int32, (NODES, NODES), 1)
    half = i // 128
    inner = i % 128
    side = jnp.where(half == 0, 1 - core, core)
    wanted = (inner // group) * (2 * group) + side * group + inner % group
    return jnp.where(c == wanted, 1.0, 0.0).astype(BF16)


def inverse_root(total, factor):
    return lax.rsqrt(total * (1.0 / (NODES * factor * factor)) + epsilon / (factor * factor))


def energy_rows(y, o):
    to_target = 1.0 / (SCENARIOS * NODES)
    between = 1.0 / (SCENARIOS * (SCENARIOS - 1) * NODES)

    def pull(a, b, factor):
        d0 = a[0] - b[0]
        d1 = a[1] - b[1]
        weight = inverse_root(jnp.sum(d0 * d0 + d1 * d1, axis=1, keepdims=True), factor)
        return weight * d0, weight * d1

    result = [pull(y[s], o, to_target) for s in range(SCENARIOS)]
    for s in range(SCENARIOS):
        for r in range(s + 1, SCENARIOS):
            p0, p1 = pull(y[s], y[r], between)
            result[s] = (result[s][0] - p0, result[s][1] - p1)
            result[r] = (result[r][0] + p0, result[r][1] + p1)
    return [jnp.concatenate(pair, axis=1) for pair in result]


def forward_kernel(
    place, from_prev, from_next, cov_hbm, obs_hbm, w_in_hbm, w_f_hbm, w_m_hbm, w_out_hbm,
    tanh_hbm, gate_hbm, dpred_hbm, cov_t_hbm, gated_t_hbm, last_t_hbm, taps_t_hbm,
    pred, target, cov, obs, w_in, w_f, w_m, w_out,
    tanh_out, gate_out, dpred, cov_t, gated_t, last_t, taps_t, sems, out_sems,
):
    cov_copy = pltpu.make_async_copy(cov_hbm, cov, sems.at[0])
    w_in_copy = pltpu.make_async_copy(w_in_hbm, w_in, sems.at[1])
    w_f_copy = pltpu.make_async_copy(w_f_hbm, w_f, sems.at[2])
    w_m_copy = pltpu.make_async_copy(w_m_hbm, w_m, sems.at[3])
    obs_copy = pltpu.make_async_copy(obs_hbm, obs, sems.at[4])
    w_out_copy = pltpu.make_async_copy(w_out_hbm, w_out, sems.at[5])
    for copy in (cov_copy, w_in_copy, w_f_copy, w_m_copy, obs_copy, w_out_copy):
        copy.start()
    core = place[0]
    perm4 = permutation(core, 4)
    perm8 = permutation(core, 8)

    def turned(perm, x):
        return mm_nt(perm, own_rows(x).astype(BF16)).astype(BF16)

    cov_copy.wait()
    pieces = []
    for b in range(SEQ):
        pieces += [
            from_prev[b].astype(F32),
            cov[b].astype(F32),
            from_next[b, :, :NODES],
        ]
    x = jnp.concatenate(pieces, axis=0)
    cov_t[...] = turned(perm4, x)
    w_in_copy.wait()
    hidden = mm(x.astype(BF16), w_in[...]).astype(BF16)
    w_f_copy.wait()
    w_m_copy.wait()
    for layer in range(LAYERS):
        wide = hidden.astype(F32)
        delayed_wide = pltpu.roll(wide, 2**layer, 0)
        delayed = delayed_wide.astype(BF16)
        taps_t[layer, 0] = turned(perm8, delayed_wide)
        taps_t[layer, 1] = turned(perm8, wide)
        preact = mm(delayed, w_f[layer, :NODES, :]) + mm(hidden, w_f[layer, NODES:, :])
        filter_act = jnp.tanh(preact[:, :NODES])
        gate_act = jax.nn.sigmoid(preact[:, NODES:])
        tanh_out[layer] = filter_act
        gate_out[layer] = gate_act
        gated = (filter_act * gate_act).astype(BF16)
        gated_t[layer] = turned(perm4, gated.astype(F32))
        hidden = (wide + mm(gated, w_m[layer])).astype(BF16)
    wide = hidden.astype(F32)
    last_t[...] = turned(perm4, wide)
    head = jnp.concatenate([wide[HALO:BLOCK], wide[BLOCK + HALO :]], axis=0).astype(BF16)
    w_out_copy.wait()
    pred[...] = mm(head, w_out[...])
    obs_copy.wait()
    for b in range(SEQ):
        target[b * HEAD : b * HEAD + ROWS, :] = obs[b]
        target[b * HEAD + ROWS : (b + 1) * HEAD, :] = from_next[b, :, NODES:]

    stores = [
        pltpu.make_async_copy(tanh_out, tanh_hbm, out_sems.at[0]),
        pltpu.make_async_copy(gate_out, gate_hbm, out_sems.at[1]),
        pltpu.make_async_copy(cov_t, cov_t_hbm, out_sems.at[2]),
        pltpu.make_async_copy(gated_t, gated_t_hbm, out_sems.at[3]),
        pltpu.make_async_copy(last_t, last_t_hbm, out_sems.at[4]),
        pltpu.make_async_copy(taps_t, taps_t_hbm, out_sems.at[5]),
    ]
    for copy in stores:
        copy.start()

    def step(i, carry):
        halves = []
        for part in range(2):
            at = pl.ds(pl.multiple_of(i * 16 + part * 8, 8), 8)
            y = [
                (pred[at, s * NODES : s * NODES + 128], pred[at, s * NODES + 128 : (s + 1) * NODES])
                for s in range(SCENARIOS)
            ]
            o = (target[at, :128], target[at, 128:])
            halves.append(energy_rows(y, o))
        at = pl.ds(pl.multiple_of(i * 16, 16), 16)
        for s in range(SCENARIOS):
            both = jnp.concatenate([halves[0][s], halves[1][s]], axis=0)
            dpred[at, s * NODES : (s + 1) * NODES] = both.astype(BF16)
        return carry

    first, last = 0, 0
    for part, last in enumerate((12, ALL_HEAD // 16)):
        lax.fori_loop(first, last, step, 0)
        rows = pl.ds(first * 16, (last - first) * 16)
        copy = pltpu.make_async_copy(dpred.at[rows], dpred_hbm.at[rows], out_sems.at[6 + part])
        copy.start()
        stores.append(copy)
        first = last
    for copy in stores:
        copy.wait()


def backward_kernel(
    place, sums, tanh_hbm, gate_hbm, dpred_hbm, cov_t_hbm, gated_t_hbm, last_t_hbm, taps_t_hbm,
    w_in_hbm, w_f_hbm, w_m_hbm, w_out_hbm,
    cov_grad, send, keep,
    tanh_in, gate_in, dpred, cov_t, gated_t, last_t, taps_t, w_in, w_f, w_m, w_out, sems,
):
    copies = [pltpu.make_async_copy(last_t_hbm, last_t, sems.at[0])]
    for x in range(4):
        columns = pl.ds(x * 1024, 1024)
        copies.append(
            pltpu.make_async_copy(dpred_hbm.at[:, columns], dpred.at[:, columns], sems.at[1 + x])
        )
    copies.append(pltpu.make_async_copy(w_out_hbm, w_out, sems.at[5]))
    later = (
        (w_m_hbm, w_m),
        (gated_t_hbm, gated_t),
        (tanh_hbm, tanh_in),
        (gate_hbm, gate_in),
        (w_f_hbm, w_f),
        (taps_t_hbm, taps_t),
        (cov_t_hbm, cov_t),
        (w_in_hbm, w_in),
    )
    for k, (source, target) in enumerate(later):
        copies.append(pltpu.make_async_copy(source, target, sems.at[6 + k]))
    for copy in copies:
        copy.start()
    copies[0].wait()
    at_end = place[1]
    steps = ROWS * place[2]
    total = jnp.sum(sums[...], axis=0)
    inv = lax.rsqrt(total / (steps * NODES).astype(F32) + epsilon)
    inv = jnp.concatenate([inv, inv], axis=1)
    for x in range(4):
        columns = slice(x * 1024, (x + 1) * 1024)
        out_grad = None
        copies[1 + x].wait()
        for b in range(SEQ):
            part = mm(
                last_t[:, b * ROWS : (b + 1) * ROWS],
                dpred[b * HEAD : b * HEAD + ROWS, columns],
            ) * inv[b : b + 1, :1]
            out_grad = part if out_grad is None else out_grad + part
        for ref, half in ((send, 0), (keep, 1)):
            for y in range(4):
                top = half * 128 + y * 32
                ref[x, y, :, :1024] = out_grad[top : top + 32].astype(BF16)
    copies[5].wait()
    head_grad = mm_nt(dpred[...], w_out[...])
    pieces = []
    for b in range(SEQ):
        scaled = head_grad[b * HEAD : (b + 1) * HEAD] * inv[b : b + 1, :]
        row = lax.broadcasted_iota(jnp.int32, (HEAD, NODES), 0)
        scaled = jnp.where((row >= ROWS) & (at_end == 1), 0.0, scaled)
        pieces += [jnp.zeros((HALO, NODES), F32), scaled]
    grad = jnp.concatenate(pieces, axis=0).astype(BF16)
    for copy in copies[6:]:
        copy.wait()
    places = ((send, 0), (keep, 1))

    def store_small(x, value):
        for ref, half in places:
            for y in range(4):
                top = half * 128 + y * 32
                ref[x, y, :, 1024:1280] = value[top : top + 32].astype(BF16)

    for layer in reversed(range(LAYERS)):
        grad_wide = grad.astype(F32)
        store_small(layer, mm(gated_t[layer], own_rows(grad_wide).astype(BF16)))
        gated_cot = mm_nt(grad, w_m[layer]).astype(BF16).astype(F32)
        filter_act = tanh_in[layer]
        gate_act = gate_in[layer]
        grad_preact = jnp.concatenate(
            [
                gated_cot * gate_act * (1.0 - filter_act * filter_act),
                gated_cot * filter_act * gate_act * (1.0 - gate_act),
            ],
            axis=1,
        )
        own_preact = own_rows(grad_preact).astype(BF16)
        grad_preact = grad_preact.astype(BF16)
        for tap in range(2):
            tap_grad = mm(taps_t[layer, tap], own_preact)
            for ref, half in places:
                for y_low in range(2):
                    top = half * 128 + y_low * 64
                    for x in range(4):
                        columns = slice(x * 128, (x + 1) * 128)
                        for low in range(2):
                            base = 1280 + low * 384 + layer * 128
                            ref[x, tap * 2 + y_low, :, base : base + 128] = tap_grad[
                                top + low * 32 : top + low * 32 + 32, columns
                            ].astype(BF16)
        grad_joined = mm_nt(grad_preact, w_f[layer]).astype(BF16)
        past = grad_joined[:, :NODES].astype(F32)
        now = grad_joined[:, NODES:].astype(F32)
        earlier = pltpu.roll(past, ALL_ROWS - 2**layer, 0)
        grad = ((grad_wide + now).astype(BF16).astype(F32) + earlier).astype(BF16)
    own = own_rows(grad.astype(F32)).astype(BF16)
    store_small(3, mm(cov_t[...], own))
    result = mm_nt(own, w_in[...]).astype(BF16)
    for b in range(SEQ):
        cov_grad[b] = result[b * ROWS : (b + 1) * ROWS]


def add_kernel(keep, got, out):
    out[...] = keep[...] + got[...]


def plane_kernel(pieces, out):
    total = pieces[0].astype(F32)
    for i in range(1, pieces.shape[0]):
        total = total + pieces[i].astype(F32)
    for z in range(8):
        r = slice(z * 4, z * 4 + 4)
        first = jnp.concatenate([total[r, :512], total[r, 1024:1152]], axis=1)
        second = jnp.concatenate([total[r, 512:1024], total[r, 1152:1280]], axis=1)
        low = z % 4
        base = 1280 + (z // 4) * 384
        taps = total[low * 8 : low * 8 + 8, base : base + 384]
        both = jnp.concatenate([first, second], axis=0)
        out[z] = jnp.concatenate([both, taps], axis=1).astype(BF16)


def line_kernel(pieces, out):
    total = pieces[0].astype(F32)
    for i in range(1, pieces.shape[0]):
        total = total + pieces[i].astype(F32)
    out[...] = total.astype(BF16)


def finish_kernel(g, input_grad, filter_grad, mixing_grad, output_grad):
    for x in range(4):
        v = g[x].astype(F32)
        output_grad[:, x * 1024 : x * 1024 + 512] = v[:4, :512].astype(BF16)
        output_grad[:, x * 1024 + 512 : (x + 1) * 1024] = v[4:, :512].astype(BF16)
        small = jnp.concatenate([v[:4, 512:640], v[4:, 512:640]], axis=1).astype(BF16)
        if x < LAYERS:
            mixing_grad[x] = small
        else:
            input_grad[...] = small
        for layer in range(LAYERS):
            base = 640 + layer * 128
            filter_grad[layer, :, x * 128 : (x + 1) * 128] = v[:, base : base + 128].astype(BF16)


BACKWARD_LIMIT = 40
HBM = pl.BlockSpec(memory_space=pltpu.HBM)
ANY = pl.BlockSpec(memory_space=pl.ANY)
SCALARS = pl.BlockSpec(memory_space=pltpu.SMEM)
WHOLE = pl.BlockSpec(memory_space=VMEM)


def call(kernel, out_shape, in_specs, scratch=(), limit=16, name=None, out_spec=WHOLE):
    return pl.pallas_call(
        kernel,
        out_shape=out_shape,
        in_specs=in_specs,
        out_specs=jax.tree.map(lambda _: out_spec, out_shape),
        scratch_shapes=scratch,
        compiler_params=pltpu.CompilerParams(vmem_limit_bytes=limit * 1024 * 1024),
        name=name,
    )


def per_device(cov, obs, w_in, w_f, w_m, w_out):
    count = lax.axis_size(TM)
    me = lax.axis_index(TM)
    place = jnp.stack(
        [
            lax.axis_index("core"),
            jnp.where(me == count - 1, 1, 0),
            jnp.int32(count),
        ]
    ).astype(jnp.int32)
    cov, obs, w_in, w_f, w_m, w_out = (
        pltpu.with_memory_space_constraint(a, pltpu.HBM) for a in (cov, obs, w_in, w_f, w_m, w_out)
    )
    to_next, to_prev, squares = call(
        start_kernel,
        (
            shape((SEQ, HALO, NODES), BF16),
            shape((SEQ, HALO, 2 * NODES), F32),
            shape((count, SEQ, 128), F32),
        ),
        [HBM, HBM],
        scratch=[
            VMEM((SEQ, 16, NODES), BF16),
            VMEM((SEQ, 16, NODES), BF16),
            VMEM(obs.shape, F32),
            pltpu.SemaphoreType.DMA((3,)),
        ],
        limit=4,
        name="start",
    )(cov, obs)
    sums = lax.all_to_all(squares, TM, 0, 0, tiled=True)
    from_prev = lax.ppermute(to_next, TM, [(i, i + 1) for i in range(count - 1)])
    from_next = lax.ppermute(to_prev, TM, [(i + 1, i) for i in range(count - 1)])

    saved_shapes = (
        pltpu.HBM((LAYERS, ALL_ROWS, NODES), F32),
        pltpu.HBM((LAYERS, ALL_ROWS, NODES), F32),
        pltpu.HBM((ALL_HEAD, SCENARIOS * NODES), BF16),
        pltpu.HBM((NODES, SEQ * ROWS), BF16),
        pltpu.HBM((LAYERS, NODES, SEQ * ROWS), BF16),
        pltpu.HBM((NODES, SEQ * ROWS), BF16),
        pltpu.HBM((LAYERS, 2, NODES, SEQ * ROWS), BF16),
    )
    saved = call(
        forward_kernel,
        saved_shapes,
        [SCALARS, WHOLE, WHOLE] + [HBM] * 6,
        scratch=[
            VMEM((ALL_HEAD, SCENARIOS * NODES), F32),
            VMEM((ALL_HEAD, NODES), F32),
            VMEM(cov.shape, BF16),
            VMEM(obs.shape, F32),
            VMEM(w_in.shape, BF16),
            VMEM(w_f.shape, BF16),
            VMEM(w_m.shape, BF16),
            VMEM(w_out.shape, BF16),
            *(VMEM(saved.shape, saved.dtype) for saved in saved_shapes),
            pltpu.SemaphoreType.DMA((6,)),
            pltpu.SemaphoreType.DMA((8,)),
        ],
        limit=40,
        name="forward",
        out_spec=HBM,
    )(place, from_prev, from_next, cov, obs, w_in, w_f, w_m, w_out)

    saved = [pltpu.with_memory_space_constraint(a, pltpu.HBM) for a in saved]
    piece = shape((4, 4, 32, 2048), BF16)
    cov_grad, send, keep = call(
        backward_kernel,
        (shape((SEQ, ROWS, NODES), BF16), piece, piece),
        [SCALARS, WHOLE] + [HBM] * 11,
        scratch=[
            *(VMEM(saved.shape, saved.dtype) for saved in saved_shapes),
            *(VMEM(w.shape, BF16) for w in (w_in, w_f, w_m, w_out)),
            pltpu.SemaphoreType.DMA((14,)),
        ],
        limit=BACKWARD_LIMIT,
        name="backward",
    )(place, sums, *saved, w_in, w_f, w_m, w_out)
    got = lax.ppermute(send, "core", [(0, 1), (1, 0)])
    chip = call(add_kernel, piece, [WHOLE] * 2, limit=4, name="pair")(keep, got)
    plane = lax.all_to_all(chip.reshape(16, 32, 2048), ("x", "y"), 0, 0, tiled=True)
    by_z = call(plane_kernel, shape((8, 8, 1024), BF16), [WHOLE], limit=4, name="plane")(plane)
    line = lax.all_to_all(by_z, "z", 0, 0, tiled=True)
    mine = call(line_kernel, shape((8, 1024), BF16), [WHOLE], limit=4, name="line")(line)
    whole = lax.all_gather(mine, "x")
    input_grad, filter_grad, mixing_grad, output_grad = call(
        finish_kernel,
        (
            shape((4, NODES), BF16),
            shape((LAYERS, 8, 2 * NODES), BF16),
            shape((LAYERS, 4, NODES), BF16),
            shape((4, SCENARIOS * NODES), BF16),
        ),
        [WHOLE],
        limit=4,
        name="finish",
    )(whole)
    return (cov_grad, input_grad, filter_grad, mixing_grad, output_grad)


def solution(mesh):
    inner = Mesh(mesh.devices.reshape(4, 8, 2, 4), ("y", "z", "core", "x"))
    data = P("x", TM, None)
    return jax.shard_map(
        per_device,
        mesh=inner,
        in_specs=(data, data, P(), P(), P(), P()),
        out_specs=(data, P(TM, None), P(None, TM, None), P(None, TM, None), P(TM, None)),
        check_vma=False,
    )
```

```python
import jax
import jax.numpy as jnp
from jax import lax
from jax.experimental import pallas as pl
from jax.experimental.pallas import tpu as pltpu
from jax.sharding import Mesh
from jax.sharding import PartitionSpec as P

epsilon = 1e-05

NODES = 256
SCENARIOS = 16
LAYERS = 3
HALO = 8
ROWS = 128
BLOCK = ROWS + 2 * HALO
SEQ = 2
ALL_ROWS = SEQ * BLOCK
OWN = SEQ * ROWS
ALL_HEAD = OWN + SEQ * HALO
TM = ("y", "z", "core")
F32 = jnp.float32
BF16 = jnp.bfloat16
VMEM = pltpu.VMEM


def mm(a, b):
    return jnp.dot(a, b, preferred_element_type=F32)


def mm_nt(a, b):
    return lax.dot_general(a, b, (((1,), (1,)), ((), ())), preferred_element_type=F32)


def shape(dims, dtype):
    return jax.ShapeDtypeStruct(dims, dtype)


def start_kernel(cov_hbm, obs_hbm, to_next, to_prev, squares, tail, head, obs, sems):
    copies = [
        pltpu.make_async_copy(obs_hbm, obs, sems.at[0]),
        pltpu.make_async_copy(cov_hbm.at[:, pl.ds(ROWS - 16, 16), :], tail, sems.at[1]),
        pltpu.make_async_copy(cov_hbm.at[:, pl.ds(0, 16), :], head, sems.at[2]),
    ]
    for copy in copies:
        copy.start()
    for copy in copies:
        copy.wait()
    for b in range(SEQ):
        to_next[b] = tail[b].astype(F32)[16 - HALO :].astype(BF16)
        to_prev[b, :, :NODES] = head[b].astype(F32)[:HALO]
        to_prev[b, :, NODES:] = obs[b, :HALO, :]
        sq = obs[b] * obs[b]
        by_lane = jnp.sum(sq, axis=0, keepdims=True)
        total = jnp.sum(by_lane, axis=1, keepdims=True)
        squares[:, b, :] = jnp.broadcast_to(total, (squares.shape[0], 128))


def own_rows(x):
    return jnp.concatenate([x[HALO : HALO + ROWS], x[BLOCK + HALO : BLOCK + HALO + ROWS]], axis=0)


def after_rows(x):
    return jnp.concatenate([x[BLOCK - HALO : BLOCK], x[2 * BLOCK - HALO :]], axis=0)


def permutation(core, group):
    i = lax.broadcasted_iota(jnp.int32, (NODES, NODES), 0)
    c = lax.broadcasted_iota(jnp.int32, (NODES, NODES), 1)
    half = i // 128
    inner = i % 128
    side = jnp.where(half == 0, 1 - core, core)
    wanted = (inner // group) * (2 * group) + side * group + inner % group
    return jnp.where(c == wanted, 1.0, 0.0).astype(BF16)


def energy_rows(y, o, scale):
    def pull(a, b):
        d0 = a[0] - b[0]
        d1 = a[1] - b[1]
        total = jnp.sum(d0 * d0 + d1 * d1, axis=1, keepdims=True)
        return d0, d1, lax.rsqrt(total + NODES * epsilon)

    result = []
    for s in range(SCENARIOS):
        d0, d1, weight = pull(y[s], o)
        weight = weight * (SCENARIOS - 1)
        result.append((weight * d0, weight * d1))
    for s in range(SCENARIOS):
        for r in range(s + 1, SCENARIOS):
            d0, d1, weight = pull(y[s], y[r])
            p0 = weight * d0
            p1 = weight * d1
            result[s] = (result[s][0] - p0, result[s][1] - p1)
            result[r] = (result[r][0] + p0, result[r][1] + p1)
    return [jnp.concatenate([scale * p0, scale * p1], axis=1) for p0, p1 in result]


def step_kernel(
    place, from_prev, from_next, sums, cov_hbm, obs_hbm, w_in_hbm, w_f_hbm, w_m_hbm, w_out_hbm,
    cov_grad, send, keep,
    pred, target, cov, obs, w_in, w_f, w_m, w_out,
    tanh_act, gate_act, dpred, cov_t, gated_t, last_t, taps_t, sems,
):
    cov_copy = pltpu.make_async_copy(cov_hbm, cov, sems.at[0])
    w_in_copy = pltpu.make_async_copy(w_in_hbm, w_in, sems.at[1])
    w_f_copy = pltpu.make_async_copy(w_f_hbm, w_f, sems.at[2])
    w_m_copy = pltpu.make_async_copy(w_m_hbm, w_m, sems.at[3])
    obs_copy = pltpu.make_async_copy(obs_hbm, obs, sems.at[4])
    w_out_copy = pltpu.make_async_copy(w_out_hbm, w_out, sems.at[5])
    for copy in (cov_copy, w_in_copy, w_f_copy, w_m_copy, obs_copy, w_out_copy):
        copy.start()
    core = place[0]
    perm4 = permutation(core, 4)
    perm8 = permutation(core, 8)

    def turned(perm, x):
        return mm_nt(perm, own_rows(x).astype(BF16)).astype(BF16)

    cov_copy.wait()
    pieces = []
    for b in range(SEQ):
        pieces += [
            from_prev[b].astype(F32),
            cov[b].astype(F32),
            from_next[b, :, :NODES],
        ]
    x = jnp.concatenate(pieces, axis=0)
    cov_t[...] = turned(perm4, x)
    w_in_copy.wait()
    hidden = mm(x.astype(BF16), w_in[...]).astype(BF16)
    w_f_copy.wait()
    w_m_copy.wait()
    for layer in range(LAYERS):
        wide = hidden.astype(F32)
        delayed_wide = pltpu.roll(wide, 2**layer, 0)
        delayed = delayed_wide.astype(BF16)
        taps_t[layer, 0] = turned(perm8, delayed_wide)
        taps_t[layer, 1] = turned(perm8, wide)
        preact = mm(delayed, w_f[layer, :NODES, :]) + mm(hidden, w_f[layer, NODES:, :])
        through = jnp.tanh(preact[:, :NODES])
        gate = jax.nn.sigmoid(preact[:, NODES:])
        tanh_act[layer] = through
        gate_act[layer] = gate
        gated = (through * gate).astype(BF16)
        gated_t[layer] = turned(perm4, gated.astype(F32))
        hidden = (wide + mm(gated, w_m[layer])).astype(BF16)
    wide = hidden.astype(F32)
    last_t[...] = turned(perm4, wide)
    head = jnp.concatenate([own_rows(wide), after_rows(wide)], axis=0).astype(BF16)
    w_out_copy.wait()
    pred[...] = mm(head, w_out[...])
    obs_copy.wait()
    for b in range(SEQ):
        target[b * ROWS : (b + 1) * ROWS, :] = obs[b]
        target[OWN + b * HALO : OWN + (b + 1) * HALO, :] = from_next[b, :, NODES:]

    at_end = place[1]
    steps = ROWS * place[2]
    total = jnp.sum(sums[...], axis=0)
    inv = lax.rsqrt(total / (steps * NODES).astype(F32) + epsilon)
    inv = inv * (NODES**0.5 / (SCENARIOS * (SCENARIOS - 1) * NODES))

    def step(i, carry):
        halves = []
        for part in range(2):
            chunk = i * 2 + part
            first = (chunk < ROWS // 8) | (chunk == OWN // 8)
            beyond = (chunk >= OWN // 8) & (at_end == 1)
            scale = jnp.where(beyond, 0.0, jnp.where(first, inv[0:1], inv[1:2]))
            at = pl.ds(pl.multiple_of(chunk * 8, 8), 8)
            y = [
                (pred[at, s * NODES : s * NODES + 128], pred[at, s * NODES + 128 : (s + 1) * NODES])
                for s in range(SCENARIOS)
            ]
            o = (target[at, :128], target[at, 128:])
            halves.append(energy_rows(y, o, scale))
        at = pl.ds(pl.multiple_of(i * 16, 16), 16)
        for s in range(SCENARIOS):
            both = jnp.concatenate([halves[0][s], halves[1][s]], axis=0)
            dpred[at, s * NODES : (s + 1) * NODES] = both.astype(BF16)
        return carry

    lax.fori_loop(0, ALL_HEAD // 16, step, 0)

    places = ((send, 0), (keep, 1))
    for x in range(4):
        out_grad = mm(last_t[...], dpred[:OWN, x * 1024 : (x + 1) * 1024])
        for ref, half in places:
            for y in range(4):
                top = half * 128 + y * 32
                ref[x, y, :, :1024] = out_grad[top : top + 32].astype(BF16)
    head_grad = mm_nt(dpred[...], w_out[...])
    pieces = []
    for b in range(SEQ):
        pieces += [
            jnp.zeros((HALO, NODES), F32),
            head_grad[b * ROWS : (b + 1) * ROWS],
            head_grad[OWN + b * HALO : OWN + (b + 1) * HALO],
        ]
    grad = jnp.concatenate(pieces, axis=0).astype(BF16)

    def store_small(x, value):
        for ref, half in places:
            for y in range(4):
                top = half * 128 + y * 32
                ref[x, y, :, 1024:1280] = value[top : top + 32].astype(BF16)

    for layer in reversed(range(LAYERS)):
        grad_wide = grad.astype(F32)
        store_small(layer, mm(gated_t[layer], own_rows(grad_wide).astype(BF16)))
        gated_cot = mm_nt(grad, w_m[layer]).astype(BF16).astype(F32)
        through = tanh_act[layer]
        gate = gate_act[layer]
        grad_preact = jnp.concatenate(
            [
                gated_cot * gate * (1.0 - through * through),
                gated_cot * through * gate * (1.0 - gate),
            ],
            axis=1,
        )
        own_preact = own_rows(grad_preact).astype(BF16)
        grad_preact = grad_preact.astype(BF16)
        for tap in range(2):
            tap_grad = mm(taps_t[layer, tap], own_preact)
            for ref, half in places:
                for y_low in range(2):
                    top = half * 128 + y_low * 64
                    for x in range(4):
                        columns = slice(x * 128, (x + 1) * 128)
                        for low in range(2):
                            base = 1280 + low * 384 + layer * 128
                            ref[x, tap * 2 + y_low, :, base : base + 128] = tap_grad[
                                top + low * 32 : top + low * 32 + 32, columns
                            ].astype(BF16)
        grad_joined = mm_nt(grad_preact, w_f[layer]).astype(BF16)
        past = grad_joined[:, :NODES].astype(F32)
        now = grad_joined[:, NODES:].astype(F32)
        earlier = pltpu.roll(past, ALL_ROWS - 2**layer, 0)
        grad = ((grad_wide + now).astype(BF16).astype(F32) + earlier).astype(BF16)
    own = own_rows(grad.astype(F32)).astype(BF16)
    store_small(3, mm(cov_t[...], own))
    result = mm_nt(own, w_in[...]).astype(BF16)
    for b in range(SEQ):
        cov_grad[b] = result[b * ROWS : (b + 1) * ROWS]


def add_kernel(keep, got, out):
    out[...] = keep[...] + got[...]


def plane_kernel(pieces, out):
    total = pieces[0].astype(F32)
    for i in range(1, pieces.shape[0]):
        total = total + pieces[i].astype(F32)
    for z in range(8):
        r = slice(z * 4, z * 4 + 4)
        first = jnp.concatenate([total[r, :512], total[r, 1024:1152]], axis=1)
        second = jnp.concatenate([total[r, 512:1024], total[r, 1152:1280]], axis=1)
        low = z % 4
        base = 1280 + (z // 4) * 384
        taps = total[low * 8 : low * 8 + 8, base : base + 384]
        both = jnp.concatenate([first, second], axis=0)
        out[z] = jnp.concatenate([both, taps], axis=1).astype(BF16)


def line_kernel(pieces, out):
    total = pieces[0].astype(F32)
    for i in range(1, pieces.shape[0]):
        total = total + pieces[i].astype(F32)
    out[...] = total.astype(BF16)


def finish_kernel(g, input_grad, filter_grad, mixing_grad, output_grad):
    for x in range(4):
        v = g[x].astype(F32)
        output_grad[:, x * 1024 : x * 1024 + 512] = v[:4, :512].astype(BF16)
        output_grad[:, x * 1024 + 512 : (x + 1) * 1024] = v[4:, :512].astype(BF16)
        small = jnp.concatenate([v[:4, 512:640], v[4:, 512:640]], axis=1).astype(BF16)
        if x < LAYERS:
            mixing_grad[x] = small
        else:
            input_grad[...] = small
        for layer in range(LAYERS):
            base = 640 + layer * 128
            filter_grad[layer, :, x * 128 : (x + 1) * 128] = v[:, base : base + 128].astype(BF16)


HBM = pl.BlockSpec(memory_space=pltpu.HBM)
ANY = pl.BlockSpec(memory_space=pl.ANY)
SCALARS = pl.BlockSpec(memory_space=pltpu.SMEM)
WHOLE = pl.BlockSpec(memory_space=VMEM)


def call(kernel, out_shape, in_specs, scratch=(), limit=16, name=None):
    return pl.pallas_call(
        kernel,
        out_shape=out_shape,
        in_specs=in_specs,
        out_specs=jax.tree.map(lambda _: WHOLE, out_shape),
        scratch_shapes=scratch,
        compiler_params=pltpu.CompilerParams(vmem_limit_bytes=limit * 1024 * 1024),
        name=name,
    )


def per_device(cov, obs, w_in, w_f, w_m, w_out):
    count = lax.axis_size(TM)
    me = lax.axis_index(TM)
    place = jnp.stack(
        [
            lax.axis_index("core"),
            jnp.where(me == count - 1, 1, 0),
            jnp.int32(count),
        ]
    ).astype(jnp.int32)
    cov, obs, w_in, w_f, w_m, w_out = (
        pltpu.with_memory_space_constraint(a, pltpu.HBM) for a in (cov, obs, w_in, w_f, w_m, w_out)
    )
    to_next, to_prev, squares = call(
        start_kernel,
        (
            shape((SEQ, HALO, NODES), BF16),
            shape((SEQ, HALO, 2 * NODES), F32),
            shape((count, SEQ, 128), F32),
        ),
        [HBM, HBM],
        scratch=[
            VMEM((SEQ, 16, NODES), BF16),
            VMEM((SEQ, 16, NODES), BF16),
            VMEM(obs.shape, F32),
            pltpu.SemaphoreType.DMA((3,)),
        ],
        limit=4,
        name="start",
    )(cov, obs)
    sums = lax.all_to_all(squares, TM, 0, 0, tiled=True)
    from_prev = lax.ppermute(to_next, TM, [(i, i + 1) for i in range(count - 1)])
    from_next = lax.ppermute(to_prev, TM, [(i + 1, i) for i in range(count - 1)])

    piece = shape((4, 4, 32, 2048), BF16)
    cov_grad, send, keep = call(
        step_kernel,
        (shape((SEQ, ROWS, NODES), BF16), piece, piece),
        [SCALARS, WHOLE, WHOLE, WHOLE] + [HBM] * 6,
        scratch=[
            VMEM((ALL_HEAD, SCENARIOS * NODES), F32),
            VMEM((ALL_HEAD, NODES), F32),
            VMEM(cov.shape, BF16),
            VMEM(obs.shape, F32),
            VMEM(w_in.shape, BF16),
            VMEM(w_f.shape, BF16),
            VMEM(w_m.shape, BF16),
            VMEM(w_out.shape, BF16),
            VMEM((LAYERS, ALL_ROWS, NODES), F32),
            VMEM((LAYERS, ALL_ROWS, NODES), F32),
            VMEM((ALL_HEAD, SCENARIOS * NODES), BF16),
            VMEM((NODES, OWN), BF16),
            VMEM((LAYERS, NODES, OWN), BF16),
            VMEM((NODES, OWN), BF16),
            VMEM((LAYERS, 2, NODES, OWN), BF16),
            pltpu.SemaphoreType.DMA((6,)),
        ],
        limit=44,
        name="step",
    )(place, from_prev, from_next, sums, cov, obs, w_in, w_f, w_m, w_out)
    got = lax.ppermute(send, "core", [(0, 1), (1, 0)])
    chip = call(add_kernel, piece, [WHOLE] * 2, limit=4, name="pair")(keep, got)
    plane = lax.all_to_all(chip.reshape(16, 32, 2048), ("x", "y"), 0, 0, tiled=True)
    by_z = call(plane_kernel, shape((8, 8, 1024), BF16), [WHOLE], limit=4, name="plane")(plane)
    line = lax.all_to_all(by_z, "z", 0, 0, tiled=True)
    mine = call(line_kernel, shape((8, 1024), BF16), [WHOLE], limit=4, name="line")(line)
    whole = lax.all_gather(mine, "x")
    input_grad, filter_grad, mixing_grad, output_grad = call(
        finish_kernel,
        (
            shape((4, NODES), BF16),
            shape((LAYERS, 8, 2 * NODES), BF16),
            shape((LAYERS, 4, NODES), BF16),
            shape((4, SCENARIOS * NODES), BF16),
        ),
        [WHOLE],
        limit=4,
        name="finish",
    )(whole)
    return (cov_grad, input_grad, filter_grad, mixing_grad, output_grad)


def solution(mesh):
    inner = Mesh(mesh.devices.reshape(4, 8, 2, 4), ("y", "z", "core", "x"))
    data = P("x", TM, None)
    return jax.shard_map(
        per_device,
        mesh=inner,
        in_specs=(data, data, P(), P(), P(), P()),
        out_specs=(data, P(TM, None), P(None, TM, None), P(None, TM, None), P(TM, None)),
        check_vma=False,
    )
```

```python
import jax
import jax.numpy as jnp
from jax import lax
from jax.experimental import pallas as pl
from jax.experimental.pallas import tpu as pltpu
from jax.sharding import Mesh
from jax.sharding import PartitionSpec as P

epsilon = 1e-05

NODES = 256
SCENARIOS = 16
LAYERS = 3
HALO = 8
ROWS = 128
BLOCK = HALO + ROWS
SEQ = 2
ALL_ROWS = SEQ * BLOCK
OWN = SEQ * ROWS
EDGE = 16
TM = ("y", "z", "core")
F32 = jnp.float32
BF16 = jnp.bfloat16
VMEM = pltpu.VMEM


def mm(a, b):
    return jnp.dot(a, b, preferred_element_type=F32)


def mm_nt(a, b):
    return lax.dot_general(a, b, (((1,), (1,)), ((), ())), preferred_element_type=F32)


def shape(dims, dtype):
    return jax.ShapeDtypeStruct(dims, dtype)


def start_kernel(cov_hbm, obs_hbm, to_next, squares, tail, obs, sems):
    copies = [
        pltpu.make_async_copy(obs_hbm, obs, sems.at[0]),
        pltpu.make_async_copy(cov_hbm.at[:, pl.ds(ROWS - EDGE, EDGE), :], tail, sems.at[1]),
    ]
    for copy in copies:
        copy.start()
    for copy in copies:
        copy.wait()
    for b in range(SEQ):
        to_next[b] = tail[b].astype(F32)[EDGE - HALO :].astype(BF16)
        mine = obs[b * ROWS : (b + 1) * ROWS]
        sq = mine * mine
        by_lane = jnp.sum(sq, axis=0, keepdims=True)
        total = jnp.sum(by_lane, axis=1, keepdims=True)
        squares[:, b, :] = jnp.broadcast_to(total, (squares.shape[0], 128))


def own_rows(x):
    return jnp.concatenate([x[HALO:BLOCK], x[BLOCK + HALO :]], axis=0)


def arranged(x):
    return jnp.concatenate([own_rows(x), x[:HALO], x[BLOCK : BLOCK + HALO]], axis=0)


def permutation(core, group):
    i = lax.broadcasted_iota(jnp.int32, (NODES, NODES), 0)
    c = lax.broadcasted_iota(jnp.int32, (NODES, NODES), 1)
    half = i // 128
    inner = i % 128
    side = jnp.where(half == 0, 1 - core, core)
    wanted = (inner // group) * (2 * group) + side * group + inner % group
    return jnp.where(c == wanted, 1.0, 0.0).astype(BF16)


def energy_rows(y, o, scale):
    def pull(a, b):
        d0 = a[0] - b[0]
        d1 = a[1] - b[1]
        total = jnp.sum(d0 * d0 + d1 * d1, axis=1, keepdims=True)
        return d0, d1, lax.rsqrt(total + NODES * epsilon)

    result = []
    for s in range(SCENARIOS):
        d0, d1, weight = pull(y[s], o)
        weight = weight * (SCENARIOS - 1)
        result.append((weight * d0, weight * d1))
    for s in range(SCENARIOS):
        for r in range(s + 1, SCENARIOS):
            d0, d1, weight = pull(y[s], y[r])
            p0 = weight * d0
            p1 = weight * d1
            result[s] = (result[s][0] - p0, result[s][1] - p1)
            result[r] = (result[r][0] + p0, result[r][1] + p1)
    return [jnp.concatenate([scale * p0, scale * p1], axis=1) for p0, p1 in result]


def step_kernel(
    place, from_prev, sums, cov_hbm, obs_hbm, w_in_hbm, w_f_hbm, w_m_hbm, w_out_hbm,
    cov_grad, last_grad, back, send, keep,
    pred, cov, obs, w_in, w_f, w_m, w_out,
    tanh_act, gate_act, dpred, cov_t, gated_t, last_t, taps_t, sems,
):
    cov_copy = pltpu.make_async_copy(cov_hbm, cov, sems.at[0])
    w_in_copy = pltpu.make_async_copy(w_in_hbm, w_in, sems.at[1])
    w_f_copy = pltpu.make_async_copy(w_f_hbm, w_f, sems.at[2])
    w_m_copy = pltpu.make_async_copy(w_m_hbm, w_m, sems.at[3])
    obs_copy = pltpu.make_async_copy(obs_hbm, obs, sems.at[4])
    w_out_copy = pltpu.make_async_copy(w_out_hbm, w_out, sems.at[5])
    for copy in (cov_copy, w_in_copy, w_f_copy, w_m_copy, obs_copy, w_out_copy):
        copy.start()
    core = place[0]
    perm4 = permutation(core, 4)
    perm8 = permutation(core, 8)

    def turned(perm, x):
        return mm_nt(perm, arranged(x).astype(BF16)).astype(BF16)

    cov_copy.wait()
    pieces = []
    for b in range(SEQ):
        pieces += [from_prev[b].astype(F32), cov[b].astype(F32)]
    x = jnp.concatenate(pieces, axis=0)
    cov_t[...] = turned(perm4, x)
    w_in_copy.wait()
    hidden = mm(x.astype(BF16), w_in[...]).astype(BF16)
    w_f_copy.wait()
    w_m_copy.wait()
    for layer in range(LAYERS):
        wide = hidden.astype(F32)
        delayed_wide = pltpu.roll(wide, 2**layer, 0)
        delayed = delayed_wide.astype(BF16)
        taps_t[layer, 0] = turned(perm8, delayed_wide)
        taps_t[layer, 1] = turned(perm8, wide)
        preact = mm(delayed, w_f[layer, :NODES, :]) + mm(hidden, w_f[layer, NODES:, :])
        through = jnp.tanh(preact[:, :NODES])
        gate = jax.nn.sigmoid(preact[:, NODES:])
        tanh_act[layer] = through
        gate_act[layer] = gate
        gated = (through * gate).astype(BF16)
        gated_t[layer] = turned(perm4, gated.astype(F32))
        hidden = (wide + mm(gated, w_m[layer])).astype(BF16)
    wide = hidden.astype(F32)
    head = own_rows(wide).astype(BF16)
    last_t[...] = mm_nt(perm4, head).astype(BF16)
    w_out_copy.wait()
    pred[...] = mm(head, w_out[...])
    obs_copy.wait()

    steps = ROWS * place[1]
    total = jnp.sum(sums[...], axis=0)
    inv = lax.rsqrt(total / (steps * NODES).astype(F32) + epsilon)
    inv = inv * (NODES**0.5 / (SCENARIOS * (SCENARIOS - 1) * NODES))

    def step(i, carry):
        halves = []
        for part in range(2):
            chunk = i * 2 + part
            scale = jnp.where(chunk < ROWS // 8, inv[0:1], inv[1:2])
            at = pl.ds(pl.multiple_of(chunk * 8, 8), 8)
            y = [
                (pred[at, s * NODES : s * NODES + 128], pred[at, s * NODES + 128 : (s + 1) * NODES])
                for s in range(SCENARIOS)
            ]
            o = (obs[at, :128], obs[at, 128:])
            halves.append(energy_rows(y, o, scale))
        at = pl.ds(pl.multiple_of(i * 16, 16), 16)
        for s in range(SCENARIOS):
            both = jnp.concatenate([halves[0][s], halves[1][s]], axis=0)
            dpred[at, s * NODES : (s + 1) * NODES] = both.astype(BF16)
        return carry

    lax.fori_loop(0, OWN // 16, step, 0)

    places = ((send, 0), (keep, 1))
    for x in range(4):
        out_grad = mm(last_t[...], dpred[:, x * 1024 : (x + 1) * 1024])
        for ref, half in places:
            for y in range(4):
                top = half * 128 + y * 32
                ref[x, y, :, :1024] = out_grad[top : top + 32].astype(BF16)
    head_grad = mm_nt(dpred[...], w_out[...])
    pieces = []
    for b in range(SEQ):
        pieces += [jnp.zeros((HALO, NODES), F32), head_grad[b * ROWS : (b + 1) * ROWS]]
    grad = jnp.concatenate(pieces, axis=0).astype(BF16)

    def store_small(x, value):
        for ref, half in places:
            for y in range(4):
                top = half * 128 + y * 32
                ref[x, y, :, 1024:1280] = value[top : top + 32].astype(BF16)

    for layer in reversed(range(LAYERS)):
        grad_wide = grad.astype(F32)
        used = OWN if layer == LAYERS - 1 else ALL_ROWS
        store_small(layer, mm(gated_t[layer, :, :used], arranged(grad_wide)[:used].astype(BF16)))
        gated_cot = mm_nt(grad, w_m[layer]).astype(BF16).astype(F32)
        through = tanh_act[layer]
        gate = gate_act[layer]
        grad_preact = jnp.concatenate(
            [
                gated_cot * gate * (1.0 - through * through),
                gated_cot * through * gate * (1.0 - gate),
            ],
            axis=1,
        )
        used_preact = arranged(grad_preact)[:used].astype(BF16)
        grad_preact = grad_preact.astype(BF16)
        for tap in range(2):
            tap_grad = mm(taps_t[layer, tap, :, :used], used_preact)
            for ref, half in places:
                for y_low in range(2):
                    top = half * 128 + y_low * 64
                    for x in range(4):
                        columns = slice(x * 128, (x + 1) * 128)
                        for low in range(2):
                            base = 1280 + low * 384 + layer * 128
                            ref[x, tap * 2 + y_low, :, base : base + 128] = tap_grad[
                                top + low * 32 : top + low * 32 + 32, columns
                            ].astype(BF16)
        grad_joined = mm_nt(grad_preact, w_f[layer]).astype(BF16)
        past = grad_joined[:, :NODES].astype(F32)
        now = grad_joined[:, NODES:].astype(F32)
        earlier = pltpu.roll(past, ALL_ROWS - 2**layer, 0)
        grad = ((grad_wide + now).astype(BF16).astype(F32) + earlier).astype(BF16)
    wide = arranged(grad.astype(F32))
    store_small(3, mm(cov_t[...], wide.astype(BF16)))
    result = mm_nt(wide[:OWN].astype(BF16), w_in[...]).astype(BF16)
    for b in range(SEQ):
        cov_grad[b] = result[b * ROWS : (b + 1) * ROWS]
        last_grad[b] = wide[(b + 1) * ROWS - EDGE : (b + 1) * ROWS].astype(BF16)
        back[b] = wide[OWN + b * HALO : OWN + (b + 1) * HALO].astype(BF16)


def add_kernel(keep, got, out):
    out[...] = keep[...] + got[...]


def plane_kernel(pieces, out):
    total = pieces[0].astype(F32)
    for i in range(1, pieces.shape[0]):
        total = total + pieces[i].astype(F32)
    for z in range(8):
        r = slice(z * 4, z * 4 + 4)
        first = jnp.concatenate([total[r, :512], total[r, 1024:1152]], axis=1)
        second = jnp.concatenate([total[r, 512:1024], total[r, 1152:1280]], axis=1)
        low = z % 4
        base = 1280 + (z // 4) * 384
        taps = total[low * 8 : low * 8 + 8, base : base + 384]
        both = jnp.concatenate([first, second], axis=0)
        out[z] = jnp.concatenate([both, taps], axis=1).astype(BF16)


def line_kernel(pieces, out):
    total = pieces[0].astype(F32)
    for i in range(1, pieces.shape[0]):
        total = total + pieces[i].astype(F32)
    for x in range(out.shape[0]):
        out[x] = total.astype(BF16)


def finish_kernel(
    g, last_grad, returned, w_in, cov_part, input_grad, filter_grad, mixing_grad, output_grad, cov_grad,
    edge, sem,
):
    rows = []
    for b in range(SEQ):
        late = last_grad[b].astype(F32)
        rows += [late[: EDGE - HALO], late[EDGE - HALO :] + returned[b].astype(F32)]
    result = mm_nt(jnp.concatenate(rows, axis=0).astype(BF16), w_in[...]).astype(BF16)
    for b in range(SEQ):
        edge[b] = result[b * EDGE : (b + 1) * EDGE]
    copy = pltpu.make_async_copy(edge, cov_grad.at[:, pl.ds(ROWS - EDGE, EDGE), :], sem)
    copy.start()
    for x in range(4):
        v = g[x].astype(F32)
        output_grad[:, x * 1024 : x * 1024 + 512] = v[:4, :512].astype(BF16)
        output_grad[:, x * 1024 + 512 : (x + 1) * 1024] = v[4:, :512].astype(BF16)
        small = jnp.concatenate([v[:4, 512:640], v[4:, 512:640]], axis=1).astype(BF16)
        if x < LAYERS:
            mixing_grad[x] = small
        else:
            input_grad[...] = small
        for layer in range(LAYERS):
            base = 640 + layer * 128
            filter_grad[layer, :, x * 128 : (x + 1) * 128] = v[:, base : base + 128].astype(BF16)
    copy.wait()


HBM = pl.BlockSpec(memory_space=pltpu.HBM)
ANY = pl.BlockSpec(memory_space=pl.ANY)
SCALARS = pl.BlockSpec(memory_space=pltpu.SMEM)
WHOLE = pl.BlockSpec(memory_space=VMEM)


def call(kernel, out_shape, in_specs, scratch=(), limit=16, name=None, out_specs=None, aliases={}):
    if out_specs is None:
        out_specs = jax.tree.map(lambda _: WHOLE, out_shape)
    return pl.pallas_call(
        kernel,
        out_shape=out_shape,
        in_specs=in_specs,
        out_specs=out_specs,
        scratch_shapes=scratch,
        input_output_aliases=aliases,
        compiler_params=pltpu.CompilerParams(vmem_limit_bytes=limit * 1024 * 1024),
        name=name,
    )


def per_device(cov, obs, w_in, w_f, w_m, w_out):
    count = lax.axis_size(TM)
    place = jnp.stack([lax.axis_index("core"), jnp.int32(count)]).astype(jnp.int32)
    obs = obs.reshape(OWN, NODES)
    cov, obs, w_in, w_f, w_m, w_out = (
        pltpu.with_memory_space_constraint(a, pltpu.HBM) for a in (cov, obs, w_in, w_f, w_m, w_out)
    )
    to_next, squares = call(
        start_kernel,
        (shape((SEQ, HALO, NODES), BF16), shape((count, SEQ, 128), F32)),
        [HBM, HBM],
        scratch=[
            VMEM((SEQ, EDGE, NODES), BF16),
            VMEM(obs.shape, F32),
            pltpu.SemaphoreType.DMA((2,)),
        ],
        limit=4,
        name="start",
    )(cov, obs)
    sums = lax.all_to_all(squares, TM, 0, 0, tiled=True)
    from_prev = lax.ppermute(to_next, TM, [(i, i + 1) for i in range(count - 1)])

    piece = shape((4, 4, 32, 2048), BF16)
    cov_part, last_grad, back, send, keep = call(
        step_kernel,
        (
            shape((SEQ, ROWS, NODES), BF16),
            shape((SEQ, EDGE, NODES), BF16),
            shape((SEQ, HALO, NODES), BF16),
            piece,
            piece,
        ),
        [SCALARS, WHOLE, WHOLE] + [HBM] * 6,
        scratch=[
            VMEM((OWN, SCENARIOS * NODES), F32),
            VMEM(cov.shape, BF16),
            VMEM((OWN, NODES), F32),
            VMEM(w_in.shape, BF16),
            VMEM(w_f.shape, BF16),
            VMEM(w_m.shape, BF16),
            VMEM(w_out.shape, BF16),
            VMEM((LAYERS, ALL_ROWS, NODES), F32),
            VMEM((LAYERS, ALL_ROWS, NODES), F32),
            VMEM((OWN, SCENARIOS * NODES), BF16),
            VMEM((NODES, ALL_ROWS), BF16),
            VMEM((LAYERS, NODES, ALL_ROWS), BF16),
            VMEM((NODES, OWN), BF16),
            VMEM((LAYERS, 2, NODES, ALL_ROWS), BF16),
            pltpu.SemaphoreType.DMA((6,)),
        ],
        limit=44,
        name="step",
    )(place, from_prev, sums, cov, obs, w_in, w_f, w_m, w_out)
    got = lax.ppermute(send, "core", [(0, 1), (1, 0)])
    returned = lax.ppermute(back, TM, [(i + 1, i) for i in range(count - 1)])
    chip = call(add_kernel, piece, [WHOLE] * 2, limit=4, name="pair")(keep, got)
    plane = lax.all_to_all(chip.reshape(16, 32, 2048), ("x", "y"), 0, 0, tiled=True)
    by_z = call(plane_kernel, shape((8, 8, 1024), BF16), [WHOLE], limit=4, name="plane")(plane)
    line = lax.all_to_all(by_z, "z", 0, 0, tiled=True)
    mine = call(line_kernel, shape((4, 8, 1024), BF16), [WHOLE], limit=4, name="line")(line)
    whole = lax.all_to_all(mine, "x", 0, 0, tiled=True)
    cov_part = pltpu.with_memory_space_constraint(cov_part, pltpu.HBM)
    input_grad, filter_grad, mixing_grad, output_grad, cov_grad = call(
        finish_kernel,
        (
            shape((4, NODES), BF16),
            shape((LAYERS, 8, 2 * NODES), BF16),
            shape((LAYERS, 4, NODES), BF16),
            shape((4, SCENARIOS * NODES), BF16),
            pltpu.HBM((SEQ, ROWS, NODES), BF16),
        ),
        [WHOLE, WHOLE, WHOLE, WHOLE, HBM],
        scratch=[VMEM((SEQ, EDGE, NODES), BF16), pltpu.SemaphoreType.DMA],
        limit=4,
        name="finish",
        out_specs=(WHOLE, WHOLE, WHOLE, WHOLE, HBM),
        aliases={4: 4},
    )(whole, last_grad, returned, w_in, cov_part)
    return (cov_grad, input_grad, filter_grad, mixing_grad, output_grad)


def solution(mesh):
    inner = Mesh(mesh.devices.reshape(4, 8, 2, 4), ("y", "z", "core", "x"))
    data = P("x", TM, None)
    return jax.shard_map(
        per_device,
        mesh=inner,
        in_specs=(data, data, P(), P(), P(), P()),
        out_specs=(data, P(TM, None), P(None, TM, None), P(None, TM, None), P(TM, None)),
        check_vma=False,
    )
```

```python
import jax
import jax.numpy as jnp
from jax import lax
from jax.experimental import pallas as pl
from jax.experimental.pallas import tpu as pltpu
from jax.sharding import Mesh
from jax.sharding import PartitionSpec as P

epsilon = 1e-05

NODES = 256
SCENARIOS = 16
LAYERS = 3
HALO = 8
ROWS = 128
BLOCK = HALO + ROWS
SEQ = 2
ALL_ROWS = SEQ * BLOCK
OWN = SEQ * ROWS
EDGE = 16
TM = ("y", "z", "core")
F32 = jnp.float32
BF16 = jnp.bfloat16
VMEM = pltpu.VMEM


def mm(a, b):
    return jnp.dot(a, b, preferred_element_type=F32)


def mm_nt(a, b):
    return lax.dot_general(a, b, (((1,), (1,)), ((), ())), preferred_element_type=F32)


def shape(dims, dtype):
    return jax.ShapeDtypeStruct(dims, dtype)


def start_kernel(cov_hbm, obs_hbm, to_next, squares, tail, obs, sems):
    copies = [
        pltpu.make_async_copy(obs_hbm, obs, sems.at[0]),
        pltpu.make_async_copy(cov_hbm.at[:, pl.ds(ROWS - EDGE, EDGE), :], tail, sems.at[1]),
    ]
    for copy in copies:
        copy.start()
    for copy in copies:
        copy.wait()
    for b in range(SEQ):
        to_next[b] = tail[b].astype(F32)[EDGE - HALO :].astype(BF16)
        mine = obs[b * ROWS : (b + 1) * ROWS]
        sq = mine * mine
        by_lane = jnp.sum(sq, axis=0, keepdims=True)
        total = jnp.sum(by_lane, axis=1, keepdims=True)
        squares[:, b, :] = jnp.broadcast_to(total, (squares.shape[0], 128))


def own_rows(x):
    return jnp.concatenate([x[HALO:BLOCK], x[BLOCK + HALO :]], axis=0)


def arranged(x):
    return jnp.concatenate([own_rows(x), x[:HALO], x[BLOCK : BLOCK + HALO]], axis=0)


def permutation(core, group):
    i = lax.broadcasted_iota(jnp.int32, (NODES, NODES), 0)
    c = lax.broadcasted_iota(jnp.int32, (NODES, NODES), 1)
    half = i // 128
    inner = i % 128
    side = jnp.where(half == 0, 1 - core, core)
    wanted = (inner // group) * (2 * group) + side * group + inner % group
    return jnp.where(c == wanted, 1.0, 0.0).astype(BF16)


def energy_rows(y, o, scale):
    def pull(a, b):
        d0 = a[0] - b[0]
        d1 = a[1] - b[1]
        total = jnp.sum(d0 * d0 + d1 * d1, axis=1, keepdims=True)
        return d0, d1, lax.rsqrt(total + NODES * epsilon)

    result = []
    for s in range(SCENARIOS):
        d0, d1, weight = pull(y[s], o)
        weight = weight * (SCENARIOS - 1)
        result.append((weight * d0, weight * d1))
    for s in range(SCENARIOS):
        for r in range(s + 1, SCENARIOS):
            d0, d1, weight = pull(y[s], y[r])
            p0 = weight * d0
            p1 = weight * d1
            result[s] = (result[s][0] - p0, result[s][1] - p1)
            result[r] = (result[r][0] + p0, result[r][1] + p1)
    return [jnp.concatenate([scale * p0, scale * p1], axis=1) for p0, p1 in result]


def step_kernel(
    place, from_prev, sums, cov_hbm, obs_hbm, w_in_hbm, w_f_hbm, w_m_hbm, w_out_hbm,
    cov_grad, last_grad, back, send, keep,
    pred, cov, obs, w_in, w_f, w_m, w_out,
    tanh_act, gate_act, dpred, cov_t, gated_t, last_t, taps_t, sems,
):
    cov_copy = pltpu.make_async_copy(cov_hbm, cov, sems.at[0])
    w_in_copy = pltpu.make_async_copy(w_in_hbm, w_in, sems.at[1])
    w_f_copy = pltpu.make_async_copy(w_f_hbm, w_f, sems.at[2])
    w_m_copy = pltpu.make_async_copy(w_m_hbm, w_m, sems.at[3])
    obs_copy = pltpu.make_async_copy(obs_hbm, obs, sems.at[4])
    w_out_copy = pltpu.make_async_copy(w_out_hbm, w_out, sems.at[5])
    for copy in (cov_copy, w_in_copy, w_f_copy, w_m_copy, obs_copy, w_out_copy):
        copy.start()
    core = place[0]
    perm4 = permutation(core, 4)
    perm8 = permutation(core, 8)

    def turned(perm, x):
        return mm_nt(perm, arranged(x).astype(BF16)).astype(BF16)

    cov_copy.wait()
    pieces = []
    for b in range(SEQ):
        pieces += [from_prev[b].astype(F32), cov[b].astype(F32)]
    x = jnp.concatenate(pieces, axis=0)
    cov_t[...] = turned(perm4, x)
    w_in_copy.wait()
    hidden = mm(x.astype(BF16), w_in[...]).astype(BF16)
    w_f_copy.wait()
    w_m_copy.wait()
    for layer in range(LAYERS):
        wide = hidden.astype(F32)
        delayed_wide = pltpu.roll(wide, 2**layer, 0)
        delayed = delayed_wide.astype(BF16)
        taps_t[layer, 0] = turned(perm8, delayed_wide)
        taps_t[layer, 1] = turned(perm8, wide)
        preact = mm(delayed, w_f[layer, :NODES, :]) + mm(hidden, w_f[layer, NODES:, :])
        through = jnp.tanh(preact[:, :NODES])
        gate = jax.nn.sigmoid(preact[:, NODES:])
        tanh_act[layer] = through
        gate_act[layer] = gate
        gated = (through * gate).astype(BF16)
        gated_t[layer] = turned(perm4, gated.astype(F32))
        hidden = (wide + mm(gated, w_m[layer])).astype(BF16)
    wide = hidden.astype(F32)
    head = own_rows(wide).astype(BF16)
    last_t[...] = mm_nt(perm4, head).astype(BF16)
    w_out_copy.wait()
    pred[...] = mm(head, w_out[...])
    obs_copy.wait()

    steps = ROWS * place[1]
    total = jnp.sum(sums[...], axis=0)
    inv = lax.rsqrt(total / (steps * NODES).astype(F32) + epsilon)
    inv = inv * (NODES**0.5 / (SCENARIOS * (SCENARIOS - 1) * NODES))

    def step(i, carry):
        halves = []
        for part in range(2):
            chunk = i * 2 + part
            scale = jnp.where(chunk < ROWS // 8, inv[0:1], inv[1:2])
            at = pl.ds(pl.multiple_of(chunk * 8, 8), 8)
            y = [
                (pred[at, s * NODES : s * NODES + 128], pred[at, s * NODES + 128 : (s + 1) * NODES])
                for s in range(SCENARIOS)
            ]
            o = (obs[at, :128], obs[at, 128:])
            halves.append(energy_rows(y, o, scale))
        at = pl.ds(pl.multiple_of(i * 16, 16), 16)
        for s in range(SCENARIOS):
            both = jnp.concatenate([halves[0][s], halves[1][s]], axis=0)
            dpred[at, s * NODES : (s + 1) * NODES] = both.astype(BF16)
        return carry

    lax.fori_loop(0, OWN // 16, step, 0)

    places = ((send, 0), (keep, 1))
    for x in range(4):
        out_grad = mm(last_t[...], dpred[:, x * 1024 : (x + 1) * 1024])
        for ref, half in places:
            for y in range(4):
                top = half * 128 + y * 32
                ref[x, y, :, :1024] = out_grad[top : top + 32].astype(BF16)
    head_grad = mm_nt(dpred[...], w_out[...])
    pieces = []
    for b in range(SEQ):
        pieces += [jnp.zeros((HALO, NODES), F32), head_grad[b * ROWS : (b + 1) * ROWS]]
    grad = jnp.concatenate(pieces, axis=0).astype(BF16)

    def store_small(x, value):
        for ref, half in places:
            for y in range(4):
                top = half * 128 + y * 32
                ref[x, y, :, 1024:1280] = value[top : top + 32].astype(BF16)

    for layer in reversed(range(LAYERS)):
        grad_wide = grad.astype(F32)
        used = OWN if layer == LAYERS - 1 else ALL_ROWS
        store_small(layer, mm(gated_t[layer, :, :used], arranged(grad_wide)[:used].astype(BF16)))
        gated_cot = mm_nt(grad, w_m[layer]).astype(BF16).astype(F32)
        through = tanh_act[layer]
        gate = gate_act[layer]
        grad_preact = jnp.concatenate(
            [
                gated_cot * gate * (1.0 - through * through),
                gated_cot * through * gate * (1.0 - gate),
            ],
            axis=1,
        )
        used_preact = arranged(grad_preact)[:used].astype(BF16)
        grad_preact = grad_preact.astype(BF16)
        for tap in range(2):
            tap_grad = mm(taps_t[layer, tap, :, :used], used_preact)
            for ref, half in places:
                for y_low in range(2):
                    top = half * 128 + y_low * 64
                    for x in range(4):
                        columns = slice(x * 128, (x + 1) * 128)
                        for low in range(2):
                            base = 1280 + low * 384 + layer * 128
                            ref[x, tap * 2 + y_low, :, base : base + 128] = tap_grad[
                                top + low * 32 : top + low * 32 + 32, columns
                            ].astype(BF16)
        grad_joined = mm_nt(grad_preact, w_f[layer]).astype(BF16)
        past = grad_joined[:, :NODES].astype(F32)
        now = grad_joined[:, NODES:].astype(F32)
        earlier = pltpu.roll(past, ALL_ROWS - 2**layer, 0)
        grad = ((grad_wide + now).astype(BF16).astype(F32) + earlier).astype(BF16)
    wide = arranged(grad.astype(F32))
    store_small(3, mm(cov_t[...], wide.astype(BF16)))
    result = mm_nt(wide[:OWN].astype(BF16), w_in[...]).astype(BF16)
    for b in range(SEQ):
        cov_grad[b] = result[b * ROWS : (b + 1) * ROWS]
        last_grad[b] = wide[(b + 1) * ROWS - EDGE : (b + 1) * ROWS].astype(BF16)
        back[b] = wide[OWN + b * HALO : OWN + (b + 1) * HALO].astype(BF16)


def pair_kernel(keep, got, last_grad, returned, w_in, cov_part, out, cov_grad, edge, sem):
    rows = []
    for b in range(SEQ):
        late = last_grad[b].astype(F32)
        rows += [late[: EDGE - HALO], late[EDGE - HALO :] + returned[b].astype(F32)]
    result = mm_nt(jnp.concatenate(rows, axis=0).astype(BF16), w_in[...]).astype(BF16)
    for b in range(SEQ):
        edge[b] = result[b * EDGE : (b + 1) * EDGE]
    copy = pltpu.make_async_copy(edge, cov_grad.at[:, pl.ds(ROWS - EDGE, EDGE), :], sem)
    copy.start()
    out[...] = keep[...] + got[...]
    copy.wait()


def plane_kernel(pieces, out):
    total = pieces[0].astype(F32)
    for i in range(1, pieces.shape[0]):
        total = total + pieces[i].astype(F32)
    for z in range(8):
        r = slice(z * 4, z * 4 + 4)
        first = jnp.concatenate([total[r, :512], total[r, 1024:1152]], axis=1)
        second = jnp.concatenate([total[r, 512:1024], total[r, 1152:1280]], axis=1)
        low = z % 4
        base = 1280 + (z // 4) * 384
        taps = total[low * 8 : low * 8 + 8, base : base + 384]
        both = jnp.concatenate([first, second], axis=0)
        out[z] = jnp.concatenate([both, taps], axis=1).astype(BF16)


def line_kernel(pieces, out):
    total = pieces[0].astype(F32)
    for i in range(1, pieces.shape[0]):
        total = total + pieces[i].astype(F32)
    for x in range(out.shape[0]):
        out[x] = total.astype(BF16)


def finish_kernel(g, input_grad, filter_grad, mixing_grad, output_grad):
    for x in range(4):
        v = g[x].astype(F32)
        output_grad[:, x * 1024 : x * 1024 + 512] = v[:4, :512].astype(BF16)
        output_grad[:, x * 1024 + 512 : (x + 1) * 1024] = v[4:, :512].astype(BF16)
        small = jnp.concatenate([v[:4, 512:640], v[4:, 512:640]], axis=1).astype(BF16)
        if x < LAYERS:
            mixing_grad[x] = small
        else:
            input_grad[...] = small
        for layer in range(LAYERS):
            base = 640 + layer * 128
            filter_grad[layer, :, x * 128 : (x + 1) * 128] = v[:, base : base + 128].astype(BF16)


HBM = pl.BlockSpec(memory_space=pltpu.HBM)
ANY = pl.BlockSpec(memory_space=pl.ANY)
SCALARS = pl.BlockSpec(memory_space=pltpu.SMEM)
WHOLE = pl.BlockSpec(memory_space=VMEM)


def call(kernel, out_shape, in_specs, scratch=(), limit=16, name=None, out_specs=None, aliases={}):
    if out_specs is None:
        out_specs = jax.tree.map(lambda _: WHOLE, out_shape)
    return pl.pallas_call(
        kernel,
        out_shape=out_shape,
        in_specs=in_specs,
        out_specs=out_specs,
        scratch_shapes=scratch,
        input_output_aliases=aliases,
        compiler_params=pltpu.CompilerParams(vmem_limit_bytes=limit * 1024 * 1024),
        name=name,
    )


def per_device(cov, obs, w_in, w_f, w_m, w_out):
    count = lax.axis_size(TM)
    place = jnp.stack([lax.axis_index("core"), jnp.int32(count)]).astype(jnp.int32)
    obs = obs.reshape(OWN, NODES)
    cov, obs, w_in, w_f, w_m, w_out = (
        pltpu.with_memory_space_constraint(a, pltpu.HBM) for a in (cov, obs, w_in, w_f, w_m, w_out)
    )
    to_next, squares = call(
        start_kernel,
        (shape((SEQ, HALO, NODES), BF16), shape((count, SEQ, 128), F32)),
        [HBM, HBM],
        scratch=[
            VMEM((SEQ, EDGE, NODES), BF16),
            VMEM(obs.shape, F32),
            pltpu.SemaphoreType.DMA((2,)),
        ],
        limit=4,
        name="start",
    )(cov, obs)
    sums = lax.all_to_all(squares, TM, 0, 0, tiled=True)
    from_prev = lax.ppermute(to_next, TM, [(i, i + 1) for i in range(count - 1)])

    piece = shape((4, 4, 32, 2048), BF16)
    cov_part, last_grad, back, send, keep = call(
        step_kernel,
        (
            shape((SEQ, ROWS, NODES), BF16),
            shape((SEQ, EDGE, NODES), BF16),
            shape((SEQ, HALO, NODES), BF16),
            piece,
            piece,
        ),
        [SCALARS, WHOLE, WHOLE] + [HBM] * 6,
        scratch=[
            VMEM((OWN, SCENARIOS * NODES), F32),
            VMEM(cov.shape, BF16),
            VMEM((OWN, NODES), F32),
            VMEM(w_in.shape, BF16),
            VMEM(w_f.shape, BF16),
            VMEM(w_m.shape, BF16),
            VMEM(w_out.shape, BF16),
            VMEM((LAYERS, ALL_ROWS, NODES), F32),
            VMEM((LAYERS, ALL_ROWS, NODES), F32),
            VMEM((OWN, SCENARIOS * NODES), BF16),
            VMEM((NODES, ALL_ROWS), BF16),
            VMEM((LAYERS, NODES, ALL_ROWS), BF16),
            VMEM((NODES, OWN), BF16),
            VMEM((LAYERS, 2, NODES, ALL_ROWS), BF16),
            pltpu.SemaphoreType.DMA((6,)),
        ],
        limit=44,
        name="step",
    )(place, from_prev, sums, cov, obs, w_in, w_f, w_m, w_out)
    got = lax.ppermute(send, "core", [(0, 1), (1, 0)])
    returned = lax.ppermute(back, TM, [(i + 1, i) for i in range(count - 1)])
    cov_part = pltpu.with_memory_space_constraint(cov_part, pltpu.HBM)
    chip, cov_grad = call(
        pair_kernel,
        (piece, pltpu.HBM((SEQ, ROWS, NODES), BF16)),
        [WHOLE] * 5 + [HBM],
        scratch=[VMEM((SEQ, EDGE, NODES), BF16), pltpu.SemaphoreType.DMA],
        limit=4,
        name="pair",
        out_specs=(WHOLE, HBM),
        aliases={5: 1},
    )(keep, got, last_grad, returned, w_in, cov_part)
    plane = lax.all_to_all(chip.reshape(16, 32, 2048), ("x", "y"), 0, 0, tiled=True)
    by_z = call(plane_kernel, shape((8, 8, 1024), BF16), [WHOLE], limit=4, name="plane")(plane)
    line = lax.all_to_all(by_z, "z", 0, 0, tiled=True)
    mine = call(line_kernel, shape((4, 8, 1024), BF16), [WHOLE], limit=4, name="line")(line)
    whole = lax.all_to_all(mine, "x", 0, 0, tiled=True)
    input_grad, filter_grad, mixing_grad, output_grad = call(
        finish_kernel,
        (
            shape((4, NODES), BF16),
            shape((LAYERS, 8, 2 * NODES), BF16),
            shape((LAYERS, 4, NODES), BF16),
            shape((4, SCENARIOS * NODES), BF16),
        ),
        [WHOLE],
        limit=4,
        name="finish",
    )(whole)
    return (cov_grad, input_grad, filter_grad, mixing_grad, output_grad)


def solution(mesh):
    inner = Mesh(mesh.devices.reshape(4, 8, 2, 4), ("y", "z", "core", "x"))
    data = P("x", TM, None)
    return jax.shard_map(
        per_device,
        mesh=inner,
        in_specs=(data, data, P(), P(), P(), P()),
        out_specs=(data, P(TM, None), P(None, TM, None), P(None, TM, None), P(TM, None)),
        check_vma=False,
    )
```

```python
import jax
import jax.numpy as jnp
from jax import lax
from jax.experimental import pallas as pl
from jax.experimental.pallas import tpu as pltpu
from jax.sharding import Mesh
from jax.sharding import PartitionSpec as P

epsilon = 1e-05

NODES = 256
SCENARIOS = 16
LAYERS = 3
HALO = 8
ROWS = 128
BLOCK = ROWS + 2 * HALO
SEQ = 2
ALL_ROWS = SEQ * BLOCK
OWN = SEQ * ROWS
ALL_HEAD = OWN + SEQ * HALO
TM = ("y", "z", "core")
F32 = jnp.float32
BF16 = jnp.bfloat16
VMEM = pltpu.VMEM


def mm(a, b):
    return jnp.dot(a, b, preferred_element_type=F32)


def mm_nt(a, b):
    return lax.dot_general(a, b, (((1,), (1,)), ((), ())), preferred_element_type=F32)


def shape(dims, dtype):
    return jax.ShapeDtypeStruct(dims, dtype)


def start_kernel(place, cov_hbm, obs_hbm, to_pair, to_far, squares, tail, head, obs, sems):
    copies = [
        pltpu.make_async_copy(obs_hbm, obs, sems.at[0]),
        pltpu.make_async_copy(cov_hbm.at[:, pl.ds(ROWS - 16, 16), :], tail, sems.at[1]),
        pltpu.make_async_copy(cov_hbm.at[:, pl.ds(0, 16), :], head, sems.at[2]),
    ]
    for copy in copies:
        copy.start()
    for copy in copies:
        copy.wait()
    first_core = place[0] == 0
    for b in range(SEQ):
        late = jnp.concatenate([tail[b].astype(F32)[16 - HALO :], obs[b, ROWS - HALO :, :]], axis=1)
        early = jnp.concatenate([head[b].astype(F32)[:HALO], obs[b, :HALO, :]], axis=1)
        to_pair[b] = jnp.where(first_core, late, early)
        to_far[b] = jnp.where(first_core, early, late)
        sq = obs[b] * obs[b]
        by_lane = jnp.sum(sq, axis=0, keepdims=True)
        total = jnp.sum(by_lane, axis=1, keepdims=True)
        squares[:, b, :] = jnp.broadcast_to(total, (squares.shape[0], 128))


def own_rows(x):
    return jnp.concatenate([x[HALO : HALO + ROWS], x[BLOCK + HALO : BLOCK + HALO + ROWS]], axis=0)


def after_rows(x):
    return jnp.concatenate([x[BLOCK - HALO : BLOCK], x[2 * BLOCK - HALO :]], axis=0)


def permutation(core, group):
    i = lax.broadcasted_iota(jnp.int32, (NODES, NODES), 0)
    c = lax.broadcasted_iota(jnp.int32, (NODES, NODES), 1)
    half = i // 128
    inner = i % 128
    side = jnp.where(half == 0, 1 - core, core)
    wanted = (inner // group) * (2 * group) + side * group + inner % group
    return jnp.where(c == wanted, 1.0, 0.0).astype(BF16)


def energy_rows(y, o, scale):
    def pull(a, b):
        d0 = a[0] - b[0]
        d1 = a[1] - b[1]
        total = jnp.sum(d0 * d0 + d1 * d1, axis=1, keepdims=True)
        return d0, d1, lax.rsqrt(total + NODES * epsilon)

    result = []
    for s in range(SCENARIOS):
        d0, d1, weight = pull(y[s], o)
        weight = weight * (SCENARIOS - 1)
        result.append((weight * d0, weight * d1))
    for s in range(SCENARIOS):
        for r in range(s + 1, SCENARIOS):
            d0, d1, weight = pull(y[s], y[r])
            p0 = weight * d0
            p1 = weight * d1
            result[s] = (result[s][0] - p0, result[s][1] - p1)
            result[r] = (result[r][0] + p0, result[r][1] + p1)
    return [jnp.concatenate([scale * p0, scale * p1], axis=1) for p0, p1 in result]


def step_kernel(
    place, from_pair, from_far, sums, cov_hbm, obs_hbm, w_in_hbm, w_f_hbm, w_m_hbm, w_out_hbm,
    cov_grad, send, keep,
    pred, target, cov, obs, w_in, w_f, w_m, w_out,
    tanh_act, gate_act, dpred, cov_t, gated_t, last_t, taps_t, sems,
):
    cov_copy = pltpu.make_async_copy(cov_hbm, cov, sems.at[0])
    w_in_copy = pltpu.make_async_copy(w_in_hbm, w_in, sems.at[1])
    w_f_copy = pltpu.make_async_copy(w_f_hbm, w_f, sems.at[2])
    w_m_copy = pltpu.make_async_copy(w_m_hbm, w_m, sems.at[3])
    obs_copy = pltpu.make_async_copy(obs_hbm, obs, sems.at[4])
    w_out_copy = pltpu.make_async_copy(w_out_hbm, w_out, sems.at[5])
    for copy in (cov_copy, w_in_copy, w_f_copy, w_m_copy, obs_copy, w_out_copy):
        copy.start()
    core = place[0]
    perm4 = permutation(core, 4)
    perm8 = permutation(core, 8)

    def turned(perm, x):
        return mm_nt(perm, own_rows(x).astype(BF16)).astype(BF16)

    cov_copy.wait()
    first_core = core == 0
    pieces = []
    for b in range(SEQ):
        before = jnp.where(first_core, from_far[b, :, :NODES], from_pair[b, :, :NODES])
        after = jnp.where(first_core, from_pair[b, :, :NODES], from_far[b, :, :NODES])
        pieces += [before, cov[b].astype(F32), after]
    x = jnp.concatenate(pieces, axis=0)
    cov_t[...] = turned(perm4, x)
    w_in_copy.wait()
    hidden = mm(x.astype(BF16), w_in[...]).astype(BF16)
    w_f_copy.wait()
    w_m_copy.wait()
    for layer in range(LAYERS):
        wide = hidden.astype(F32)
        delayed_wide = pltpu.roll(wide, 2**layer, 0)
        delayed = delayed_wide.astype(BF16)
        taps_t[layer, 0] = turned(perm8, delayed_wide)
        taps_t[layer, 1] = turned(perm8, wide)
        preact = mm(delayed, w_f[layer, :NODES, :]) + mm(hidden, w_f[layer, NODES:, :])
        through = jnp.tanh(preact[:, :NODES])
        gate = jax.nn.sigmoid(preact[:, NODES:])
        tanh_act[layer] = through
        gate_act[layer] = gate
        gated = (through * gate).astype(BF16)
        gated_t[layer] = turned(perm4, gated.astype(F32))
        hidden = (wide + mm(gated, w_m[layer])).astype(BF16)
    wide = hidden.astype(F32)
    last_t[...] = turned(perm4, wide)
    head = jnp.concatenate([own_rows(wide), after_rows(wide)], axis=0).astype(BF16)
    w_out_copy.wait()
    pred[...] = mm(head, w_out[...])
    obs_copy.wait()
    for b in range(SEQ):
        target[b * ROWS : (b + 1) * ROWS, :] = obs[b]
        target[OWN + b * HALO : OWN + (b + 1) * HALO, :] = jnp.where(
            first_core, from_pair[b, :, NODES:], from_far[b, :, NODES:]
        )

    at_end = place[1]
    steps = ROWS * place[2]
    total = jnp.sum(sums[...], axis=0)
    inv = lax.rsqrt(total / (steps * NODES).astype(F32) + epsilon)
    inv = inv * (NODES**0.5 / (SCENARIOS * (SCENARIOS - 1) * NODES))

    def step(i, carry):
        halves = []
        for part in range(2):
            chunk = i * 2 + part
            first = (chunk < ROWS // 8) | (chunk == OWN // 8)
            beyond = (chunk >= OWN // 8) & (at_end == 1)
            scale = jnp.where(beyond, 0.0, jnp.where(first, inv[0:1], inv[1:2]))
            at = pl.ds(pl.multiple_of(chunk * 8, 8), 8)
            y = [
                (pred[at, s * NODES : s * NODES + 128], pred[at, s * NODES + 128 : (s + 1) * NODES])
                for s in range(SCENARIOS)
            ]
            o = (target[at, :128], target[at, 128:])
            halves.append(energy_rows(y, o, scale))
        at = pl.ds(pl.multiple_of(i * 16, 16), 16)
        for s in range(SCENARIOS):
            both = jnp.concatenate([halves[0][s], halves[1][s]], axis=0)
            dpred[at, s * NODES : (s + 1) * NODES] = both.astype(BF16)
        return carry

    lax.fori_loop(0, ALL_HEAD // 16, step, 0)

    places = ((send, 0), (keep, 1))
    for x in range(4):
        out_grad = mm(last_t[...], dpred[:OWN, x * 1024 : (x + 1) * 1024])
        for ref, half in places:
            for y in range(4):
                top = half * 128 + y * 32
                ref[x, y, :, :1024] = out_grad[top : top + 32].astype(BF16)
    head_grad = mm_nt(dpred[...], w_out[...])
    pieces = []
    for b in range(SEQ):
        pieces += [
            jnp.zeros((HALO, NODES), F32),
            head_grad[b * ROWS : (b + 1) * ROWS],
            head_grad[OWN + b * HALO : OWN + (b + 1) * HALO],
        ]
    grad = jnp.concatenate(pieces, axis=0).astype(BF16)

    def store_small(x, value):
        for ref, half in places:
            for y in range(4):
                top = half * 128 + y * 32
                ref[x, y, :, 1024:1280] = value[top : top + 32].astype(BF16)

    for layer in reversed(range(LAYERS)):
        grad_wide = grad.astype(F32)
        store_small(layer, mm(gated_t[layer], own_rows(grad_wide).astype(BF16)))
        gated_cot = mm_nt(grad, w_m[layer]).astype(BF16).astype(F32)
        through = tanh_act[layer]
        gate = gate_act[layer]
        grad_preact = jnp.concatenate(
            [
                gated_cot * gate * (1.0 - through * through),
                gated_cot * through * gate * (1.0 - gate),
            ],
            axis=1,
        )
        own_preact = own_rows(grad_preact).astype(BF16)
        grad_preact = grad_preact.astype(BF16)
        for tap in range(2):
            tap_grad = mm(taps_t[layer, tap], own_preact)
            for ref, half in places:
                for y_low in range(2):
                    top = half * 128 + y_low * 64
                    for x in range(4):
                        columns = slice(x * 128, (x + 1) * 128)
                        for low in range(2):
                            base = 1280 + low * 384 + layer * 128
                            ref[x, tap * 2 + y_low, :, base : base + 128] = tap_grad[
                                top + low * 32 : top + low * 32 + 32, columns
                            ].astype(BF16)
        grad_joined = mm_nt(grad_preact, w_f[layer]).astype(BF16)
        past = grad_joined[:, :NODES].astype(F32)
        now = grad_joined[:, NODES:].astype(F32)
        earlier = pltpu.roll(past, ALL_ROWS - 2**layer, 0)
        grad = ((grad_wide + now).astype(BF16).astype(F32) + earlier).astype(BF16)
    own = own_rows(grad.astype(F32)).astype(BF16)
    store_small(3, mm(cov_t[...], own))
    result = mm_nt(own, w_in[...]).astype(BF16)
    for b in range(SEQ):
        cov_grad[b] = result[b * ROWS : (b + 1) * ROWS]


def add_kernel(keep, got, out):
    out[...] = keep[...] + got[...]


def plane_kernel(pieces, out):
    total = pieces[0].astype(F32)
    for i in range(1, pieces.shape[0]):
        total = total + pieces[i].astype(F32)
    for z in range(8):
        r = slice(z * 4, z * 4 + 4)
        first = jnp.concatenate([total[r, :512], total[r, 1024:1152]], axis=1)
        second = jnp.concatenate([total[r, 512:1024], total[r, 1152:1280]], axis=1)
        low = z % 4
        base = 1280 + (z // 4) * 384
        taps = total[low * 8 : low * 8 + 8, base : base + 384]
        both = jnp.concatenate([first, second], axis=0)
        out[z] = jnp.concatenate([both, taps], axis=1).astype(BF16)


def line_kernel(pieces, out):
    total = pieces[0].astype(F32)
    for i in range(1, pieces.shape[0]):
        total = total + pieces[i].astype(F32)
    for x in range(out.shape[0]):
        out[x] = total.astype(BF16)


def finish_kernel(g, input_grad, filter_grad, mixing_grad, output_grad):
    for x in range(4):
        v = g[x].astype(F32)
        output_grad[:, x * 1024 : x * 1024 + 512] = v[:4, :512].astype(BF16)
        output_grad[:, x * 1024 + 512 : (x + 1) * 1024] = v[4:, :512].astype(BF16)
        small = jnp.concatenate([v[:4, 512:640], v[4:, 512:640]], axis=1).astype(BF16)
        if x < LAYERS:
            mixing_grad[x] = small
        else:
            input_grad[...] = small
        for layer in range(LAYERS):
            base = 640 + layer * 128
            filter_grad[layer, :, x * 128 : (x + 1) * 128] = v[:, base : base + 128].astype(BF16)


HBM = pl.BlockSpec(memory_space=pltpu.HBM)
ANY = pl.BlockSpec(memory_space=pl.ANY)
SCALARS = pl.BlockSpec(memory_space=pltpu.SMEM)
WHOLE = pl.BlockSpec(memory_space=VMEM)


def call(kernel, out_shape, in_specs, scratch=(), limit=16, name=None):
    return pl.pallas_call(
        kernel,
        out_shape=out_shape,
        in_specs=in_specs,
        out_specs=jax.tree.map(lambda _: WHOLE, out_shape),
        scratch_shapes=scratch,
        compiler_params=pltpu.CompilerParams(vmem_limit_bytes=limit * 1024 * 1024),
        name=name,
    )


def per_device(cov, obs, w_in, w_f, w_m, w_out):
    count = lax.axis_size(TM)
    me = lax.axis_index(TM)
    place = jnp.stack(
        [
            lax.axis_index("core"),
            jnp.where(me == count - 1, 1, 0),
            jnp.int32(count),
        ]
    ).astype(jnp.int32)
    cov, obs, w_in, w_f, w_m, w_out = (
        pltpu.with_memory_space_constraint(a, pltpu.HBM) for a in (cov, obs, w_in, w_f, w_m, w_out)
    )
    edge = shape((SEQ, HALO, 2 * NODES), F32)
    to_pair, to_far, squares = call(
        start_kernel,
        (edge, edge, shape((count, SEQ, 128), F32)),
        [SCALARS, HBM, HBM],
        scratch=[
            VMEM((SEQ, 16, NODES), BF16),
            VMEM((SEQ, 16, NODES), BF16),
            VMEM(obs.shape, F32),
            pltpu.SemaphoreType.DMA((3,)),
        ],
        limit=4,
        name="start",
    )(place, cov, obs)
    sums = lax.all_to_all(squares, TM, 0, 0, tiled=True)
    from_pair = lax.ppermute(to_pair, "core", [(0, 1), (1, 0)])
    seams = [(i, i + 1) for i in range(1, count - 1, 2)]
    from_far = lax.ppermute(to_far, TM, seams + [(j, i) for i, j in seams])

    piece = shape((4, 4, 32, 2048), BF16)
    cov_grad, send, keep = call(
        step_kernel,
        (shape((SEQ, ROWS, NODES), BF16), piece, piece),
        [SCALARS, WHOLE, WHOLE, WHOLE] + [HBM] * 6,
        scratch=[
            VMEM((ALL_HEAD, SCENARIOS * NODES), F32),
            VMEM((ALL_HEAD, NODES), F32),
            VMEM(cov.shape, BF16),
            VMEM(obs.shape, F32),
            VMEM(w_in.shape, BF16),
            VMEM(w_f.shape, BF16),
            VMEM(w_m.shape, BF16),
            VMEM(w_out.shape, BF16),
            VMEM((LAYERS, ALL_ROWS, NODES), F32),
            VMEM((LAYERS, ALL_ROWS, NODES), F32),
            VMEM((ALL_HEAD, SCENARIOS * NODES), BF16),
            VMEM((NODES, OWN), BF16),
            VMEM((LAYERS, NODES, OWN), BF16),
            VMEM((NODES, OWN), BF16),
            VMEM((LAYERS, 2, NODES, OWN), BF16),
            pltpu.SemaphoreType.DMA((6,)),
        ],
        limit=44,
        name="step",
    )(place, from_pair, from_far, sums, cov, obs, w_in, w_f, w_m, w_out)
    got = lax.ppermute(send, "core", [(0, 1), (1, 0)])
    chip = call(add_kernel, piece, [WHOLE] * 2, limit=4, name="pair")(keep, got)
    plane = lax.all_to_all(chip.reshape(16, 32, 2048), ("x", "y"), 0, 0, tiled=True)
    by_z = call(plane_kernel, shape((8, 8, 1024), BF16), [WHOLE], limit=4, name="plane")(plane)
    line = lax.all_to_all(by_z, "z", 0, 0, tiled=True)
    mine = call(line_kernel, shape((4, 8, 1024), BF16), [WHOLE], limit=4, name="line")(line)
    whole = lax.all_to_all(mine, "x", 0, 0, tiled=True)
    input_grad, filter_grad, mixing_grad, output_grad = call(
        finish_kernel,
        (
            shape((4, NODES), BF16),
            shape((LAYERS, 8, 2 * NODES), BF16),
            shape((LAYERS, 4, NODES), BF16),
            shape((4, SCENARIOS * NODES), BF16),
        ),
        [WHOLE],
        limit=4,
        name="finish",
    )(whole)
    return (cov_grad, input_grad, filter_grad, mixing_grad, output_grad)


def solution(mesh):
    inner = Mesh(mesh.devices.reshape(4, 8, 2, 4), ("y", "z", "core", "x"))
    data = P("x", TM, None)
    return jax.shard_map(
        per_device,
        mesh=inner,
        in_specs=(data, data, P(), P(), P(), P()),
        out_specs=(data, P(TM, None), P(None, TM, None), P(None, TM, None), P(TM, None)),
        check_vma=False,
    )
```

```python
import jax
import jax.numpy as jnp
from jax import lax
from jax.experimental import pallas as pl
from jax.experimental.pallas import tpu as pltpu
from jax.sharding import Mesh
from jax.sharding import PartitionSpec as P

epsilon = 1e-05

NODES = 256
SCENARIOS = 16
LAYERS = 3
HALO = 8
ROWS = 128
BLOCK = ROWS + 2 * HALO
SEQ = 2
ALL_ROWS = SEQ * BLOCK
OWN = SEQ * ROWS
ALL_HEAD = OWN + SEQ * HALO
TM = ("y", "z", "core")
F32 = jnp.float32
BF16 = jnp.bfloat16
VMEM = pltpu.VMEM


def mm(a, b):
    return jnp.dot(a, b, preferred_element_type=F32)


def mm_nt(a, b):
    return lax.dot_general(a, b, (((1,), (1,)), ((), ())), preferred_element_type=F32)


def shape(dims, dtype):
    return jax.ShapeDtypeStruct(dims, dtype)


def start_kernel(cov_hbm, obs_hbm, to_pair, to_far, squares, tail, head, obs, sems):
    copies = [
        pltpu.make_async_copy(obs_hbm, obs, sems.at[0]),
        pltpu.make_async_copy(cov_hbm.at[:, pl.ds(ROWS - 16, 16), :], tail, sems.at[1]),
        pltpu.make_async_copy(cov_hbm.at[:, pl.ds(0, 16), :], head, sems.at[2]),
    ]
    for copy in copies:
        copy.start()
    for copy in copies:
        copy.wait()
    first_core = lax.axis_index("core") == 0
    for b in range(SEQ):
        late = jnp.concatenate([tail[b].astype(F32)[16 - HALO :], obs[b, ROWS - HALO :, :]], axis=1)
        early = jnp.concatenate([head[b].astype(F32)[:HALO], obs[b, :HALO, :]], axis=1)
        to_pair[b] = jnp.where(first_core, late, early)
        to_far[b] = jnp.where(first_core, early, late)
        sq = obs[b] * obs[b]
        by_lane = jnp.sum(sq, axis=0, keepdims=True)
        total = jnp.sum(by_lane, axis=1, keepdims=True)
        squares[:, b, :] = jnp.broadcast_to(total, (squares.shape[0], 128))


def own_rows(x):
    return jnp.concatenate([x[HALO : HALO + ROWS], x[BLOCK + HALO : BLOCK + HALO + ROWS]], axis=0)


def after_rows(x):
    return jnp.concatenate([x[BLOCK - HALO : BLOCK], x[2 * BLOCK - HALO :]], axis=0)


def permutation(core, group):
    i = lax.broadcasted_iota(jnp.int32, (NODES, NODES), 0)
    c = lax.broadcasted_iota(jnp.int32, (NODES, NODES), 1)
    half = i // 128
    inner = i % 128
    side = jnp.where(half == 0, 1 - core, core)
    wanted = (inner // group) * (2 * group) + side * group + inner % group
    return jnp.where(c == wanted, 1.0, 0.0).astype(BF16)


def energy_rows(y, o, scale):
    def pull(a, b):
        d0 = a[0] - b[0]
        d1 = a[1] - b[1]
        total = jnp.sum(d0 * d0 + d1 * d1, axis=1, keepdims=True)
        return d0, d1, lax.rsqrt(total + NODES * epsilon)

    result = []
    for s in range(SCENARIOS):
        d0, d1, weight = pull(y[s], o)
        weight = weight * (SCENARIOS - 1)
        result.append((weight * d0, weight * d1))
    for s in range(SCENARIOS):
        for r in range(s + 1, SCENARIOS):
            d0, d1, weight = pull(y[s], y[r])
            p0 = weight * d0
            p1 = weight * d1
            result[s] = (result[s][0] - p0, result[s][1] - p1)
            result[r] = (result[r][0] + p0, result[r][1] + p1)
    return [jnp.concatenate([scale * p0, scale * p1], axis=1) for p0, p1 in result]


def score_kernel(
    from_pair, from_far, sums, cov_hbm, obs_hbm, w_in_hbm, w_f_hbm, w_m_hbm, w_out_hbm,
    grad_out, send, keep, tanh_act, gate_act, cov_t, gated_t, taps_t, w_in, w_f, w_m,
    pred, target, cov, obs, w_out, dpred, last_t, sems,
):
    cov_copy = pltpu.make_async_copy(cov_hbm, cov, sems.at[0])
    w_in_copy = pltpu.make_async_copy(w_in_hbm, w_in, sems.at[1])
    w_f_copy = pltpu.make_async_copy(w_f_hbm, w_f, sems.at[2])
    w_m_copy = pltpu.make_async_copy(w_m_hbm, w_m, sems.at[3])
    obs_copy = pltpu.make_async_copy(obs_hbm, obs, sems.at[4])
    w_out_copy = pltpu.make_async_copy(w_out_hbm, w_out, sems.at[5])
    for copy in (cov_copy, w_in_copy, w_f_copy, w_m_copy, obs_copy, w_out_copy):
        copy.start()
    core = lax.axis_index("core")
    perm4 = permutation(core, 4)
    perm8 = permutation(core, 8)

    def turned(perm, x):
        return mm_nt(perm, own_rows(x).astype(BF16)).astype(BF16)

    cov_copy.wait()
    first_core = core == 0
    pieces = []
    for b in range(SEQ):
        before = jnp.where(first_core, from_far[b, :, :NODES], from_pair[b, :, :NODES])
        after = jnp.where(first_core, from_pair[b, :, :NODES], from_far[b, :, :NODES])
        pieces += [before, cov[b].astype(F32), after]
    x = jnp.concatenate(pieces, axis=0)
    cov_t[...] = turned(perm4, x)
    w_in_copy.wait()
    hidden = mm(x.astype(BF16), w_in[...]).astype(BF16)
    w_f_copy.wait()
    w_m_copy.wait()
    for layer in range(LAYERS):
        wide = hidden.astype(F32)
        delayed_wide = pltpu.roll(wide, 2**layer, 0)
        delayed = delayed_wide.astype(BF16)
        taps_t[layer, 0] = turned(perm8, delayed_wide)
        taps_t[layer, 1] = turned(perm8, wide)
        preact = mm(delayed, w_f[layer, :NODES, :]) + mm(hidden, w_f[layer, NODES:, :])
        through = jnp.tanh(preact[:, :NODES])
        gate = jax.nn.sigmoid(preact[:, NODES:])
        tanh_act[layer] = through
        gate_act[layer] = gate
        gated = (through * gate).astype(BF16)
        gated_t[layer] = turned(perm4, gated.astype(F32))
        hidden = (wide + mm(gated, w_m[layer])).astype(BF16)
    wide = hidden.astype(F32)
    last_t[...] = turned(perm4, wide)
    head = jnp.concatenate([own_rows(wide), after_rows(wide)], axis=0).astype(BF16)
    w_out_copy.wait()
    pred[...] = mm(head, w_out[...])
    obs_copy.wait()
    for b in range(SEQ):
        target[b * ROWS : (b + 1) * ROWS, :] = obs[b]
        target[OWN + b * HALO : OWN + (b + 1) * HALO, :] = jnp.where(
            first_core, from_pair[b, :, NODES:], from_far[b, :, NODES:]
        )

    at_end = lax.axis_index(TM) == lax.axis_size(TM) - 1
    steps = ROWS * lax.axis_size(TM)
    total = jnp.sum(sums[...], axis=0)
    inv = lax.rsqrt(total / (steps * NODES) + epsilon)
    inv = inv * (NODES**0.5 / (SCENARIOS * (SCENARIOS - 1) * NODES))

    def step(i, carry):
        halves = []
        for part in range(2):
            chunk = i * 2 + part
            first = (chunk < ROWS // 8) | (chunk == OWN // 8)
            beyond = (chunk >= OWN // 8) & at_end
            scale = jnp.where(beyond, 0.0, jnp.where(first, inv[0:1], inv[1:2]))
            at = pl.ds(pl.multiple_of(chunk * 8, 8), 8)
            y = [
                (pred[at, s * NODES : s * NODES + 128], pred[at, s * NODES + 128 : (s + 1) * NODES])
                for s in range(SCENARIOS)
            ]
            o = (target[at, :128], target[at, 128:])
            halves.append(energy_rows(y, o, scale))
        at = pl.ds(pl.multiple_of(i * 16, 16), 16)
        for s in range(SCENARIOS):
            both = jnp.concatenate([halves[0][s], halves[1][s]], axis=0)
            dpred[at, s * NODES : (s + 1) * NODES] = both.astype(BF16)
        return carry

    lax.fori_loop(0, ALL_HEAD // 16, step, 0)

    places = ((send, 0), (keep, 1))
    for x in range(4):
        out_grad = mm(last_t[...], dpred[:OWN, x * 1024 : (x + 1) * 1024])
        for ref, half in places:
            for y in range(4):
                top = half * 128 + y * 32
                ref[x, y] = out_grad[top : top + 32].astype(BF16)
    head_grad = mm_nt(dpred[...], w_out[...])
    pieces = []
    for b in range(SEQ):
        pieces += [
            jnp.zeros((HALO, NODES), F32),
            head_grad[b * ROWS : (b + 1) * ROWS],
            head_grad[OWN + b * HALO : OWN + (b + 1) * HALO],
        ]
    grad_out[...] = jnp.concatenate(pieces, axis=0).astype(BF16)


def layers_kernel(
    grad_in, tanh_act, gate_act, cov_t, gated_t, taps_t, w_in, w_f, w_m,
    cov_grad, send, keep,
):
    grad = grad_in[...]
    places = ((send, 0), (keep, 1))

    def store_small(x, value):
        for ref, half in places:
            for y in range(4):
                top = half * 128 + y * 32
                ref[x, y, :, :256] = value[top : top + 32].astype(BF16)

    for layer in reversed(range(LAYERS)):
        grad_wide = grad.astype(F32)
        store_small(layer, mm(gated_t[layer], own_rows(grad_wide).astype(BF16)))
        gated_cot = mm_nt(grad, w_m[layer]).astype(BF16).astype(F32)
        through = tanh_act[layer]
        gate = gate_act[layer]
        grad_preact = jnp.concatenate(
            [
                gated_cot * gate * (1.0 - through * through),
                gated_cot * through * gate * (1.0 - gate),
            ],
            axis=1,
        )
        own_preact = own_rows(grad_preact).astype(BF16)
        grad_preact = grad_preact.astype(BF16)
        for tap in range(2):
            tap_grad = mm(taps_t[layer, tap], own_preact)
            for ref, half in places:
                for y_low in range(2):
                    top = half * 128 + y_low * 64
                    for x in range(4):
                        columns = slice(x * 128, (x + 1) * 128)
                        for low in range(2):
                            base = 256 + low * 384 + layer * 128
                            ref[x, tap * 2 + y_low, :, base : base + 128] = tap_grad[
                                top + low * 32 : top + low * 32 + 32, columns
                            ].astype(BF16)
        grad_joined = mm_nt(grad_preact, w_f[layer]).astype(BF16)
        past = grad_joined[:, :NODES].astype(F32)
        now = grad_joined[:, NODES:].astype(F32)
        earlier = pltpu.roll(past, ALL_ROWS - 2**layer, 0)
        grad = ((grad_wide + now).astype(BF16).astype(F32) + earlier).astype(BF16)
    own = own_rows(grad.astype(F32)).astype(BF16)
    store_small(3, mm(cov_t[...], own))
    result = mm_nt(own, w_in[...]).astype(BF16)
    for b in range(SEQ):
        cov_grad[b] = result[b * ROWS : (b + 1) * ROWS]


def add_kernel(keep, got, out):
    out[...] = keep[...] + got[...]


def join_kernel(score, keep, got, out):
    out[:, :, :, :1024] = score[...]
    out[:, :, :, 1024:] = keep[...] + got[...]


def plane_kernel(pieces, out):
    total = pieces[0].astype(F32)
    for i in range(1, pieces.shape[0]):
        total = total + pieces[i].astype(F32)
    for z in range(8):
        r = slice(z * 4, z * 4 + 4)
        first = jnp.concatenate([total[r, :512], total[r, 1024:1152]], axis=1)
        second = jnp.concatenate([total[r, 512:1024], total[r, 1152:1280]], axis=1)
        low = z % 4
        base = 1280 + (z // 4) * 384
        taps = total[low * 8 : low * 8 + 8, base : base + 384]
        both = jnp.concatenate([first, second], axis=0)
        out[z] = jnp.concatenate([both, taps], axis=1).astype(BF16)


def line_kernel(pieces, out):
    total = pieces[0].astype(F32)
    for i in range(1, pieces.shape[0]):
        total = total + pieces[i].astype(F32)
    for x in range(out.shape[0]):
        out[x] = total.astype(BF16)


def finish_kernel(g, input_grad, filter_grad, mixing_grad, output_grad):
    for x in range(4):
        v = g[x].astype(F32)
        output_grad[:, x * 1024 : x * 1024 + 512] = v[:4, :512].astype(BF16)
        output_grad[:, x * 1024 + 512 : (x + 1) * 1024] = v[4:, :512].astype(BF16)
        small = jnp.concatenate([v[:4, 512:640], v[4:, 512:640]], axis=1).astype(BF16)
        if x < LAYERS:
            mixing_grad[x] = small
        else:
            input_grad[...] = small
        for layer in range(LAYERS):
            base = 640 + layer * 128
            filter_grad[layer, :, x * 128 : (x + 1) * 128] = v[:, base : base + 128].astype(BF16)


HBM = pl.BlockSpec(memory_space=pltpu.HBM)
ANY = pl.BlockSpec(memory_space=pl.ANY)
WHOLE = pl.BlockSpec(memory_space=VMEM)


def call(kernel, out_shape, in_specs, scratch=(), limit=16, name=None, cost=None):
    return pl.pallas_call(
        kernel,
        out_shape=out_shape,
        in_specs=in_specs,
        out_specs=jax.tree.map(lambda _: WHOLE, out_shape),
        scratch_shapes=scratch,
        compiler_params=pltpu.CompilerParams(vmem_limit_bytes=limit * 1024 * 1024),
        name=name,
        cost_estimate=cost,
    )


def per_device(cov, obs, w_in, w_f, w_m, w_out):
    count = lax.axis_size(TM)
    cov, obs, w_in, w_f, w_m, w_out = (
        pltpu.with_memory_space_constraint(a, pltpu.HBM) for a in (cov, obs, w_in, w_f, w_m, w_out)
    )
    edge = shape((SEQ, HALO, 2 * NODES), F32)
    to_pair, to_far, squares = call(
        start_kernel,
        (edge, edge, shape((count, SEQ, 128), F32)),
        [HBM, HBM],
        scratch=[
            VMEM((SEQ, 16, NODES), BF16),
            VMEM((SEQ, 16, NODES), BF16),
            VMEM(obs.shape, F32),
            pltpu.SemaphoreType.DMA((3,)),
        ],
        limit=4,
        name="start",
    )(cov, obs)
    sums = lax.all_to_all(squares, TM, 0, 0, tiled=True)
    from_pair = lax.ppermute(to_pair, "core", [(0, 1), (1, 0)])
    seams = [(i, i + 1) for i in range(1, count - 1, 2)]
    from_far = lax.ppermute(to_far, TM, seams + [(j, i) for i, j in seams])

    part = shape((4, 4, 32, 1024), BF16)
    act = shape((LAYERS, ALL_ROWS, NODES), F32)
    grad, send_score, keep_score, *saved = call(
        score_kernel,
        (
            shape((ALL_ROWS, NODES), BF16),
            part,
            part,
            act,
            act,
            shape((NODES, OWN), BF16),
            shape((LAYERS, NODES, OWN), BF16),
            shape((LAYERS, 2, NODES, OWN), BF16),
            shape(w_in.shape, BF16),
            shape(w_f.shape, BF16),
            shape(w_m.shape, BF16),
        ),
        [WHOLE, WHOLE, WHOLE] + [HBM] * 6,
        scratch=[
            VMEM((ALL_HEAD, SCENARIOS * NODES), F32),
            VMEM((ALL_HEAD, NODES), F32),
            VMEM(cov.shape, BF16),
            VMEM(obs.shape, F32),
            VMEM(w_out.shape, BF16),
            VMEM((ALL_HEAD, SCENARIOS * NODES), BF16),
            VMEM((NODES, OWN), BF16),
            pltpu.SemaphoreType.DMA((6,)),
        ],
        limit=36,
        name="score",
        cost=pl.CostEstimate(flops=10**10, transcendentals=0, bytes_accessed=10**7),
    )(from_pair, from_far, sums, cov, obs, w_in, w_f, w_m, w_out)
    swap = [(0, 1), (1, 0)]
    got_score = lax.ppermute(send_score, "core", swap)
    cov_grad, send_rest, keep_rest = call(
        layers_kernel,
        (shape((SEQ, ROWS, NODES), BF16), part, part),
        [WHOLE] * 9,
        limit=16,
        name="layers",
        cost=pl.CostEstimate(flops=4 * 10**9, transcendentals=0, bytes_accessed=10**7),
    )(grad, *saved)
    got_rest = lax.ppermute(send_rest, "core", swap)
    score = call(add_kernel, part, [WHOLE] * 2, limit=4, name="pair")(keep_score, got_score)
    chip = call(join_kernel, shape((4, 4, 32, 2048), BF16), [WHOLE] * 3, limit=4, name="join")(
        score, keep_rest, got_rest
    )
    plane = lax.all_to_all(chip.reshape(16, 32, 2048), ("x", "y"), 0, 0, tiled=True)
    by_z = call(plane_kernel, shape((8, 8, 1024), BF16), [WHOLE], limit=4, name="plane")(plane)
    line = lax.all_to_all(by_z, "z", 0, 0, tiled=True)
    mine = call(line_kernel, shape((4, 8, 1024), BF16), [WHOLE], limit=4, name="line")(line)
    whole = lax.all_to_all(mine, "x", 0, 0, tiled=True)
    input_grad, filter_grad, mixing_grad, output_grad = call(
        finish_kernel,
        (
            shape((4, NODES), BF16),
            shape((LAYERS, 8, 2 * NODES), BF16),
            shape((LAYERS, 4, NODES), BF16),
            shape((4, SCENARIOS * NODES), BF16),
        ),
        [WHOLE],
        limit=4,
        name="finish",
    )(whole)
    return (cov_grad, input_grad, filter_grad, mixing_grad, output_grad)


def solution(mesh):
    inner = Mesh(mesh.devices.reshape(4, 8, 2, 4), ("y", "z", "core", "x"))
    data = P("x", TM, None)
    return jax.shard_map(
        per_device,
        mesh=inner,
        in_specs=(data, data, P(), P(), P(), P()),
        out_specs=(data, P(TM, None), P(None, TM, None), P(None, TM, None), P(TM, None)),
        check_vma=False,
    )
```

```python
import jax
import jax.numpy as jnp
from jax import lax
from jax.experimental import pallas as pl
from jax.experimental.pallas import tpu as pltpu
from jax.sharding import Mesh
from jax.sharding import PartitionSpec as P

epsilon = 1e-05

NODES = 256
SCENARIOS = 16
LAYERS = 3
HALO = 8
ROWS = 128
BLOCK = ROWS + 2 * HALO
SEQ = 2
ALL_ROWS = SEQ * BLOCK
OWN = SEQ * ROWS
ALL_HEAD = OWN + SEQ * HALO
TM = ("y", "z", "core")
F32 = jnp.float32
BF16 = jnp.bfloat16
VMEM = pltpu.VMEM


def mm(a, b):
    return jnp.dot(a, b, preferred_element_type=F32)


def mm_nt(a, b):
    return lax.dot_general(a, b, (((1,), (1,)), ((), ())), preferred_element_type=F32)


def shape(dims, dtype):
    return jax.ShapeDtypeStruct(dims, dtype)


def start_kernel(cov_hbm, obs_hbm, to_pair, to_far, squares, tail, head, obs, sems):
    copies = [
        pltpu.make_async_copy(obs_hbm, obs, sems.at[0]),
        pltpu.make_async_copy(cov_hbm.at[:, pl.ds(ROWS - 16, 16), :], tail, sems.at[1]),
        pltpu.make_async_copy(cov_hbm.at[:, pl.ds(0, 16), :], head, sems.at[2]),
    ]
    for copy in copies:
        copy.start()
    for copy in copies:
        copy.wait()
    first_core = lax.axis_index("core") == 0
    for b in range(SEQ):
        late = jnp.concatenate([tail[b].astype(F32)[16 - HALO :], obs[b, ROWS - HALO :, :]], axis=1)
        early = jnp.concatenate([head[b].astype(F32)[:HALO], obs[b, :HALO, :]], axis=1)
        to_pair[b] = jnp.where(first_core, late, early)
        to_far[b] = jnp.where(first_core, early, late)
        sq = obs[b] * obs[b]
        by_lane = jnp.sum(sq, axis=0, keepdims=True)
        total = jnp.sum(by_lane, axis=1, keepdims=True)
        squares[:, b, :] = jnp.broadcast_to(total, (squares.shape[0], 128))


def own_rows(x):
    return jnp.concatenate([x[HALO : HALO + ROWS], x[BLOCK + HALO : BLOCK + HALO + ROWS]], axis=0)


def after_rows(x):
    return jnp.concatenate([x[BLOCK - HALO : BLOCK], x[2 * BLOCK - HALO :]], axis=0)


def permutation(core, group):
    i = lax.broadcasted_iota(jnp.int32, (NODES, NODES), 0)
    c = lax.broadcasted_iota(jnp.int32, (NODES, NODES), 1)
    half = i // 128
    inner = i % 128
    side = jnp.where(half == 0, 1 - core, core)
    wanted = (inner // group) * (2 * group) + side * group + inner % group
    return jnp.where(c == wanted, 1.0, 0.0).astype(BF16)


def energy_rows(y, o, scale):
    def pull(a, b):
        d0 = a[0] - b[0]
        d1 = a[1] - b[1]
        total = jnp.sum(d0 * d0 + d1 * d1, axis=1, keepdims=True)
        return d0, d1, lax.rsqrt(total + NODES * epsilon)

    result = []
    for s in range(SCENARIOS):
        d0, d1, weight = pull(y[s], o)
        weight = weight * (SCENARIOS - 1)
        result.append((weight * d0, weight * d1))
    for s in range(SCENARIOS):
        for r in range(s + 1, SCENARIOS):
            d0, d1, weight = pull(y[s], y[r])
            p0 = weight * d0
            p1 = weight * d1
            result[s] = (result[s][0] - p0, result[s][1] - p1)
            result[r] = (result[r][0] + p0, result[r][1] + p1)
    return [jnp.concatenate([scale * p0, scale * p1], axis=1) for p0, p1 in result]


def score_kernel(
    from_pair, from_far, sums, cov_hbm, obs_hbm, w_in_hbm, w_f_hbm, w_m_hbm, w_out_hbm,
    grad_out, send, keep, tanh_act, gate_act, cov_t, gated_t, taps_t, w_in, w_f, w_m,
    pred, target, cov, obs, w_out, dpred, last_t, sems,
):
    cov_copy = pltpu.make_async_copy(cov_hbm, cov, sems.at[0])
    w_in_copy = pltpu.make_async_copy(w_in_hbm, w_in, sems.at[1])
    w_f_copy = pltpu.make_async_copy(w_f_hbm, w_f, sems.at[2])
    w_m_copy = pltpu.make_async_copy(w_m_hbm, w_m, sems.at[3])
    obs_copy = pltpu.make_async_copy(obs_hbm, obs, sems.at[4])
    w_out_copy = pltpu.make_async_copy(w_out_hbm, w_out, sems.at[5])
    for copy in (cov_copy, w_in_copy, w_f_copy, w_m_copy, obs_copy, w_out_copy):
        copy.start()
    core = lax.axis_index("core")
    perm4 = permutation(core, 4)
    perm8 = permutation(core, 8)

    def turned(perm, x):
        return mm_nt(perm, own_rows(x).astype(BF16)).astype(BF16)

    cov_copy.wait()
    first_core = core == 0
    pieces = []
    for b in range(SEQ):
        before = jnp.where(first_core, from_far[b, :, :NODES], from_pair[b, :, :NODES])
        after = jnp.where(first_core, from_pair[b, :, :NODES], from_far[b, :, :NODES])
        pieces += [before, cov[b].astype(F32), after]
    x = jnp.concatenate(pieces, axis=0)
    cov_t[...] = turned(perm4, x)
    w_in_copy.wait()
    hidden = mm(x.astype(BF16), w_in[...]).astype(BF16)
    w_f_copy.wait()
    w_m_copy.wait()
    for layer in range(LAYERS):
        wide = hidden.astype(F32)
        delayed_wide = pltpu.roll(wide, 2**layer, 0)
        delayed = delayed_wide.astype(BF16)
        taps_t[layer, 0] = turned(perm8, delayed_wide)
        taps_t[layer, 1] = turned(perm8, wide)
        preact = mm(delayed, w_f[layer, :NODES, :]) + mm(hidden, w_f[layer, NODES:, :])
        through = jnp.tanh(preact[:, :NODES])
        gate = jax.nn.sigmoid(preact[:, NODES:])
        tanh_act[layer] = through
        gate_act[layer] = gate
        gated = (through * gate).astype(BF16)
        gated_t[layer] = turned(perm4, gated.astype(F32))
        hidden = (wide + mm(gated, w_m[layer])).astype(BF16)
    wide = hidden.astype(F32)
    last_t[...] = turned(perm4, wide)
    head = jnp.concatenate([own_rows(wide), after_rows(wide)], axis=0).astype(BF16)
    w_out_copy.wait()
    pred[...] = mm(head, w_out[...])
    obs_copy.wait()
    for b in range(SEQ):
        target[b * ROWS : (b + 1) * ROWS, :] = obs[b]
        target[OWN + b * HALO : OWN + (b + 1) * HALO, :] = jnp.where(
            first_core, from_pair[b, :, NODES:], from_far[b, :, NODES:]
        )

    at_end = lax.axis_index(TM) == lax.axis_size(TM) - 1
    steps = ROWS * lax.axis_size(TM)
    total = jnp.sum(sums[...], axis=0)
    inv = lax.rsqrt(total / (steps * NODES) + epsilon)
    inv = inv * (NODES**0.5 / (SCENARIOS * (SCENARIOS - 1) * NODES))

    def step(i, carry):
        halves = []
        for part in range(2):
            chunk = i * 2 + part
            first = (chunk < ROWS // 8) | (chunk == OWN // 8)
            beyond = (chunk >= OWN // 8) & at_end
            scale = jnp.where(beyond, 0.0, jnp.where(first, inv[0:1], inv[1:2]))
            at = pl.ds(pl.multiple_of(chunk * 8, 8), 8)
            y = [
                (pred[at, s * NODES : s * NODES + 128], pred[at, s * NODES + 128 : (s + 1) * NODES])
                for s in range(SCENARIOS)
            ]
            o = (target[at, :128], target[at, 128:])
            halves.append(energy_rows(y, o, scale))
        at = pl.ds(pl.multiple_of(i * 16, 16), 16)
        for s in range(SCENARIOS):
            both = jnp.concatenate([halves[0][s], halves[1][s]], axis=0)
            dpred[at, s * NODES : (s + 1) * NODES] = both.astype(BF16)
        return carry

    lax.fori_loop(0, OWN // 16, step, 0, unroll=4)
    step(OWN // 16, 0)

    places = ((send, 0), (keep, 1))
    for x in range(4):
        out_grad = mm(last_t[...], dpred[:OWN, x * 1024 : (x + 1) * 1024])
        for ref, half in places:
            for y in range(4):
                top = half * 128 + y * 32
                ref[x, y] = out_grad[top : top + 32].astype(BF16)
    head_grad = mm_nt(dpred[...], w_out[...])
    pieces = []
    for b in range(SEQ):
        pieces += [
            jnp.zeros((HALO, NODES), F32),
            head_grad[b * ROWS : (b + 1) * ROWS],
            head_grad[OWN + b * HALO : OWN + (b + 1) * HALO],
        ]
    grad_out[...] = jnp.concatenate(pieces, axis=0).astype(BF16)


def layers_kernel(
    grad_in, tanh_act, gate_act, cov_t, gated_t, taps_t, w_in, w_f, w_m,
    cov_grad, send, keep,
):
    grad = grad_in[...]
    places = ((send, 0), (keep, 1))

    def store_small(x, value):
        for ref, half in places:
            for y in range(4):
                top = half * 128 + y * 32
                ref[x, y, :, :256] = value[top : top + 32].astype(BF16)

    for layer in reversed(range(LAYERS)):
        grad_wide = grad.astype(F32)
        store_small(layer, mm(gated_t[layer], own_rows(grad_wide).astype(BF16)))
        gated_cot = mm_nt(grad, w_m[layer]).astype(BF16).astype(F32)
        through = tanh_act[layer]
        gate = gate_act[layer]
        grad_preact = jnp.concatenate(
            [
                gated_cot * gate * (1.0 - through * through),
                gated_cot * through * gate * (1.0 - gate),
            ],
            axis=1,
        )
        own_preact = own_rows(grad_preact).astype(BF16)
        grad_preact = grad_preact.astype(BF16)
        for tap in range(2):
            tap_grad = mm(taps_t[layer, tap], own_preact)
            for ref, half in places:
                for y_low in range(2):
                    top = half * 128 + y_low * 64
                    for x in range(4):
                        columns = slice(x * 128, (x + 1) * 128)
                        for low in range(2):
                            base = 256 + low * 384 + layer * 128
                            ref[x, tap * 2 + y_low, :, base : base + 128] = tap_grad[
                                top + low * 32 : top + low * 32 + 32, columns
                            ].astype(BF16)
        grad_joined = mm_nt(grad_preact, w_f[layer]).astype(BF16)
        past = grad_joined[:, :NODES].astype(F32)
        now = grad_joined[:, NODES:].astype(F32)
        earlier = pltpu.roll(past, ALL_ROWS - 2**layer, 0)
        grad = ((grad_wide + now).astype(BF16).astype(F32) + earlier).astype(BF16)
    own = own_rows(grad.astype(F32)).astype(BF16)
    store_small(3, mm(cov_t[...], own))
    result = mm_nt(own, w_in[...]).astype(BF16)
    for b in range(SEQ):
        cov_grad[b] = result[b * ROWS : (b + 1) * ROWS]


def add_kernel(keep, got, out):
    out[...] = keep[...] + got[...]


def join_kernel(score, keep, got, out):
    out[:, :, :, :1024] = score[...]
    out[:, :, :, 1024:] = keep[...] + got[...]


def plane_kernel(pieces, out):
    total = pieces[0].astype(F32)
    for i in range(1, pieces.shape[0]):
        total = total + pieces[i].astype(F32)
    for z in range(8):
        r = slice(z * 4, z * 4 + 4)
        first = jnp.concatenate([total[r, :512], total[r, 1024:1152]], axis=1)
        second = jnp.concatenate([total[r, 512:1024], total[r, 1152:1280]], axis=1)
        low = z % 4
        base = 1280 + (z // 4) * 384
        taps = total[low * 8 : low * 8 + 8, base : base + 384]
        both = jnp.concatenate([first, second], axis=0)
        out[z] = jnp.concatenate([both, taps], axis=1).astype(BF16)


def line_kernel(pieces, out):
    total = pieces[0].astype(F32)
    for i in range(1, pieces.shape[0]):
        total = total + pieces[i].astype(F32)
    for x in range(out.shape[0]):
        out[x] = total.astype(BF16)


def finish_kernel(g, input_grad, filter_grad, mixing_grad, output_grad):
    for x in range(4):
        v = g[x].astype(F32)
        output_grad[:, x * 1024 : x * 1024 + 512] = v[:4, :512].astype(BF16)
        output_grad[:, x * 1024 + 512 : (x + 1) * 1024] = v[4:, :512].astype(BF16)
        small = jnp.concatenate([v[:4, 512:640], v[4:, 512:640]], axis=1).astype(BF16)
        if x < LAYERS:
            mixing_grad[x] = small
        else:
            input_grad[...] = small
        for layer in range(LAYERS):
            base = 640 + layer * 128
            filter_grad[layer, :, x * 128 : (x + 1) * 128] = v[:, base : base + 128].astype(BF16)


HBM = pl.BlockSpec(memory_space=pltpu.HBM)
ANY = pl.BlockSpec(memory_space=pl.ANY)
WHOLE = pl.BlockSpec(memory_space=VMEM)


def call(kernel, out_shape, in_specs, scratch=(), limit=16, name=None, cost=None):
    return pl.pallas_call(
        kernel,
        out_shape=out_shape,
        in_specs=in_specs,
        out_specs=jax.tree.map(lambda _: WHOLE, out_shape),
        scratch_shapes=scratch,
        compiler_params=pltpu.CompilerParams(vmem_limit_bytes=limit * 1024 * 1024),
        name=name,
        cost_estimate=cost,
    )


def per_device(cov, obs, w_in, w_f, w_m, w_out):
    count = lax.axis_size(TM)
    cov, obs, w_in, w_f, w_m, w_out = (
        pltpu.with_memory_space_constraint(a, pltpu.HBM) for a in (cov, obs, w_in, w_f, w_m, w_out)
    )
    edge = shape((SEQ, HALO, 2 * NODES), F32)
    to_pair, to_far, squares = call(
        start_kernel,
        (edge, edge, shape((count, SEQ, 128), F32)),
        [HBM, HBM],
        scratch=[
            VMEM((SEQ, 16, NODES), BF16),
            VMEM((SEQ, 16, NODES), BF16),
            VMEM(obs.shape, F32),
            pltpu.SemaphoreType.DMA((3,)),
        ],
        limit=4,
        name="start",
    )(cov, obs)
    sums = lax.all_to_all(squares, TM, 0, 0, tiled=True)
    from_pair = lax.ppermute(to_pair, "core", [(0, 1), (1, 0)])
    seams = [(i, i + 1) for i in range(1, count - 1, 2)]
    from_far = lax.ppermute(to_far, TM, seams + [(j, i) for i, j in seams])

    part = shape((4, 4, 32, 1024), BF16)
    act = shape((LAYERS, ALL_ROWS, NODES), F32)
    grad, send_score, keep_score, *saved = call(
        score_kernel,
        (
            shape((ALL_ROWS, NODES), BF16),
            part,
            part,
            act,
            act,
            shape((NODES, OWN), BF16),
            shape((LAYERS, NODES, OWN), BF16),
            shape((LAYERS, 2, NODES, OWN), BF16),
            shape(w_in.shape, BF16),
            shape(w_f.shape, BF16),
            shape(w_m.shape, BF16),
        ),
        [WHOLE, WHOLE, WHOLE] + [HBM] * 6,
        scratch=[
            VMEM((ALL_HEAD, SCENARIOS * NODES), F32),
            VMEM((ALL_HEAD, NODES), F32),
            VMEM(cov.shape, BF16),
            VMEM(obs.shape, F32),
            VMEM(w_out.shape, BF16),
            VMEM((ALL_HEAD, SCENARIOS * NODES), BF16),
            VMEM((NODES, OWN), BF16),
            pltpu.SemaphoreType.DMA((6,)),
        ],
        limit=36,
        name="score",
        cost=pl.CostEstimate(flops=10**10, transcendentals=0, bytes_accessed=10**7),
    )(from_pair, from_far, sums, cov, obs, w_in, w_f, w_m, w_out)
    swap = [(0, 1), (1, 0)]
    got_score = lax.ppermute(send_score, "core", swap)
    cov_grad, send_rest, keep_rest = call(
        layers_kernel,
        (shape((SEQ, ROWS, NODES), BF16), part, part),
        [WHOLE] * 9,
        limit=16,
        name="layers",
        cost=pl.CostEstimate(flops=4 * 10**9, transcendentals=0, bytes_accessed=10**7),
    )(grad, *saved)
    got_rest = lax.ppermute(send_rest, "core", swap)
    score = call(add_kernel, part, [WHOLE] * 2, limit=4, name="pair")(keep_score, got_score)
    chip = call(join_kernel, shape((4, 4, 32, 2048), BF16), [WHOLE] * 3, limit=4, name="join")(
        score, keep_rest, got_rest
    )
    plane = lax.all_to_all(chip.reshape(16, 32, 2048), ("x", "y"), 0, 0, tiled=True)
    by_z = call(plane_kernel, shape((8, 8, 1024), BF16), [WHOLE], limit=4, name="plane")(plane)
    line = lax.all_to_all(by_z, "z", 0, 0, tiled=True)
    mine = call(line_kernel, shape((4, 8, 1024), BF16), [WHOLE], limit=4, name="line")(line)
    whole = lax.all_to_all(mine, "x", 0, 0, tiled=True)
    input_grad, filter_grad, mixing_grad, output_grad = call(
        finish_kernel,
        (
            shape((4, NODES), BF16),
            shape((LAYERS, 8, 2 * NODES), BF16),
            shape((LAYERS, 4, NODES), BF16),
            shape((4, SCENARIOS * NODES), BF16),
        ),
        [WHOLE],
        limit=4,
        name="finish",
    )(whole)
    return (cov_grad, input_grad, filter_grad, mixing_grad, output_grad)


def solution(mesh):
    inner = Mesh(mesh.devices.reshape(4, 8, 2, 4), ("y", "z", "core", "x"))
    data = P("x", TM, None)
    return jax.shard_map(
        per_device,
        mesh=inner,
        in_specs=(data, data, P(), P(), P(), P()),
        out_specs=(data, P(TM, None), P(None, TM, None), P(None, TM, None), P(TM, None)),
        check_vma=False,
    )
```

```python
import jax
import jax.numpy as jnp
from jax import lax
from jax.experimental import pallas as pl
from jax.experimental.pallas import tpu as pltpu
from jax.sharding import Mesh
from jax.sharding import PartitionSpec as P

epsilon = 1e-05

NODES = 256
SCENARIOS = 16
LAYERS = 3
HALO = 8
ROWS = 128
BLOCK = ROWS + 2 * HALO
SEQ = 2
ALL_ROWS = SEQ * BLOCK
OWN = SEQ * ROWS
ALL_HEAD = OWN + SEQ * HALO
TM = ("y", "z", "core")
F32 = jnp.float32
BF16 = jnp.bfloat16
VMEM = pltpu.VMEM


def mm(a, b):
    return jnp.dot(a, b, preferred_element_type=F32)


def mm_nt(a, b):
    return lax.dot_general(a, b, (((1,), (1,)), ((), ())), preferred_element_type=F32)


def shape(dims, dtype):
    return jax.ShapeDtypeStruct(dims, dtype)


def start_kernel(cov_hbm, obs_hbm, to_pair, to_far, squares, tail, head, obs, sems):
    copies = [
        pltpu.make_async_copy(obs_hbm, obs, sems.at[0]),
        pltpu.make_async_copy(cov_hbm.at[:, pl.ds(ROWS - 16, 16), :], tail, sems.at[1]),
        pltpu.make_async_copy(cov_hbm.at[:, pl.ds(0, 16), :], head, sems.at[2]),
    ]
    for copy in copies:
        copy.start()
    for copy in copies:
        copy.wait()
    first_core = lax.axis_index("core") == 0
    for b in range(SEQ):
        late = jnp.concatenate([tail[b].astype(F32)[16 - HALO :], obs[b, ROWS - HALO :, :]], axis=1)
        early = jnp.concatenate([head[b].astype(F32)[:HALO], obs[b, :HALO, :]], axis=1)
        to_pair[b] = jnp.where(first_core, late, early)
        to_far[b] = jnp.where(first_core, early, late)
        sq = obs[b] * obs[b]
        by_lane = jnp.sum(sq, axis=0, keepdims=True)
        total = jnp.sum(by_lane, axis=1, keepdims=True)
        squares[:, b, :] = jnp.broadcast_to(total, (squares.shape[0], 128))


def own_rows(x):
    return jnp.concatenate([x[HALO : HALO + ROWS], x[BLOCK + HALO : BLOCK + HALO + ROWS]], axis=0)


def after_rows(x):
    return jnp.concatenate([x[BLOCK - HALO : BLOCK], x[2 * BLOCK - HALO :]], axis=0)


def permutation(core, group):
    i = lax.broadcasted_iota(jnp.int32, (NODES, NODES), 0)
    c = lax.broadcasted_iota(jnp.int32, (NODES, NODES), 1)
    half = i // 128
    inner = i % 128
    side = jnp.where(half == 0, 1 - core, core)
    wanted = (inner // group) * (2 * group) + side * group + inner % group
    return jnp.where(c == wanted, 1.0, 0.0).astype(BF16)


def energy_rows(y, o, scale):
    def pull(a, b):
        d0 = a[0] - b[0]
        d1 = a[1] - b[1]
        total = jnp.sum(d0 * d0 + d1 * d1, axis=1, keepdims=True)
        return d0, d1, lax.rsqrt(total + NODES * epsilon)

    result = []
    for s in range(SCENARIOS):
        d0, d1, weight = pull(y[s], o)
        weight = weight * (SCENARIOS - 1)
        result.append((weight * d0, weight * d1))
    for s in range(SCENARIOS):
        for r in range(s + 1, SCENARIOS):
            d0, d1, weight = pull(y[s], y[r])
            p0 = weight * d0
            p1 = weight * d1
            result[s] = (result[s][0] - p0, result[s][1] - p1)
            result[r] = (result[r][0] + p0, result[r][1] + p1)
    return [jnp.concatenate([scale * p0, scale * p1], axis=1) for p0, p1 in result]


def score_kernel(
    from_pair, from_far, sums, cov_hbm, obs_hbm, w_in_hbm, w_f_hbm, w_m_hbm, w_out_hbm,
    grad_out, send, keep, tanh_act, gate_act, cov_t, gated_t, taps_t, w_in, w_f, w_m,
    pred, target, cov, obs, w_out, dpred, last_t, sems,
):
    cov_copy = pltpu.make_async_copy(cov_hbm, cov, sems.at[0])
    w_in_copy = pltpu.make_async_copy(w_in_hbm, w_in, sems.at[1])
    w_f_copy = pltpu.make_async_copy(w_f_hbm, w_f, sems.at[2])
    w_m_copy = pltpu.make_async_copy(w_m_hbm, w_m, sems.at[3])
    obs_copy = pltpu.make_async_copy(obs_hbm, obs, sems.at[4])
    w_out_copy = pltpu.make_async_copy(w_out_hbm, w_out, sems.at[5])
    for copy in (cov_copy, w_in_copy, w_f_copy, w_m_copy, obs_copy, w_out_copy):
        copy.start()
    core = lax.axis_index("core")
    perm4 = permutation(core, 4)
    perm8 = permutation(core, 8)

    def turned(perm, x):
        return mm_nt(perm, own_rows(x).astype(BF16)).astype(BF16)

    cov_copy.wait()
    first_core = core == 0
    pieces = []
    for b in range(SEQ):
        before = jnp.where(first_core, from_far[b, :, :NODES], from_pair[b, :, :NODES])
        after = jnp.where(first_core, from_pair[b, :, :NODES], from_far[b, :, :NODES])
        pieces += [before, cov[b].astype(F32), after]
    x = jnp.concatenate(pieces, axis=0)
    cov_t[...] = turned(perm4, x)
    w_in_copy.wait()
    hidden = mm(x.astype(BF16), w_in[...]).astype(BF16)
    w_f_copy.wait()
    w_m_copy.wait()
    for layer in range(LAYERS):
        wide = hidden.astype(F32)
        delayed_wide = pltpu.roll(wide, 2**layer, 0)
        delayed = delayed_wide.astype(BF16)
        taps_t[layer, 0] = turned(perm8, delayed_wide)
        taps_t[layer, 1] = turned(perm8, wide)
        preact = mm(delayed, w_f[layer, :NODES, :]) + mm(hidden, w_f[layer, NODES:, :])
        through = jnp.tanh(preact[:, :NODES])
        gate = jax.nn.sigmoid(preact[:, NODES:])
        tanh_act[layer] = through
        gate_act[layer] = gate
        gated = (through * gate).astype(BF16)
        gated_t[layer] = turned(perm4, gated.astype(F32))
        hidden = (wide + mm(gated, w_m[layer])).astype(BF16)
    wide = hidden.astype(F32)
    last_t[...] = turned(perm4, wide)
    head = jnp.concatenate([own_rows(wide), after_rows(wide)], axis=0).astype(BF16)
    w_out_copy.wait()
    pred[...] = mm(head, w_out[...])
    obs_copy.wait()
    for b in range(SEQ):
        target[b * ROWS : (b + 1) * ROWS, :] = obs[b]
        target[OWN + b * HALO : OWN + (b + 1) * HALO, :] = jnp.where(
            first_core, from_pair[b, :, NODES:], from_far[b, :, NODES:]
        )

    at_end = lax.axis_index(TM) == lax.axis_size(TM) - 1
    steps = ROWS * lax.axis_size(TM)
    total = jnp.sum(sums[...], axis=0)
    inv = lax.rsqrt(total / (steps * NODES) + epsilon)
    inv = inv * (NODES**0.5 / (SCENARIOS * (SCENARIOS - 1) * NODES))

    def step(i, carry):
        halves = []
        for part in range(2):
            chunk = i * 2 + part
            first = (chunk < ROWS // 8) | (chunk == OWN // 8)
            beyond = (chunk >= OWN // 8) & at_end
            scale = jnp.where(beyond, 0.0, jnp.where(first, inv[0:1], inv[1:2]))
            at = pl.ds(pl.multiple_of(chunk * 8, 8), 8)
            y = [
                (pred[at, s * NODES : s * NODES + 128], pred[at, s * NODES + 128 : (s + 1) * NODES])
                for s in range(SCENARIOS)
            ]
            o = (target[at, :128], target[at, 128:])
            halves.append(energy_rows(y, o, scale))
        at = pl.ds(pl.multiple_of(i * 16, 16), 16)
        for s in range(SCENARIOS):
            both = jnp.concatenate([halves[0][s], halves[1][s]], axis=0)
            dpred[at, s * NODES : (s + 1) * NODES] = both.astype(BF16)
        return carry

    lax.fori_loop(0, OWN // 16, step, 0, unroll=4)
    step(OWN // 16, 0)

    places = ((send, 0), (keep, 1))
    for x in range(4):
        out_grad = mm(last_t[...], dpred[:OWN, x * 1024 : (x + 1) * 1024])
        for ref, half in places:
            for y in range(4):
                top = half * 128 + y * 32
                ref[y, x] = out_grad[top : top + 32].astype(BF16)
    head_grad = mm_nt(dpred[...], w_out[...])
    pieces = []
    for b in range(SEQ):
        pieces += [
            jnp.zeros((HALO, NODES), F32),
            head_grad[b * ROWS : (b + 1) * ROWS],
            head_grad[OWN + b * HALO : OWN + (b + 1) * HALO],
        ]
    grad_out[...] = jnp.concatenate(pieces, axis=0).astype(BF16)


def layers_kernel(
    grad_in, tanh_act, gate_act, cov_t, gated_t, taps_t, w_in, w_f, w_m,
    cov_grad, send, keep,
):
    grad = grad_in[...]
    places = ((send, 0), (keep, 1))

    def store_small(x, value):
        for ref, half in places:
            for y in range(4):
                top = half * 128 + y * 32
                ref[y, x, :, :256] = value[top : top + 32].astype(BF16)

    for layer in reversed(range(LAYERS)):
        grad_wide = grad.astype(F32)
        store_small(layer, mm(gated_t[layer], own_rows(grad_wide).astype(BF16)))
        gated_cot = mm_nt(grad, w_m[layer]).astype(BF16).astype(F32)
        through = tanh_act[layer]
        gate = gate_act[layer]
        grad_preact = jnp.concatenate(
            [
                gated_cot * gate * (1.0 - through * through),
                gated_cot * through * gate * (1.0 - gate),
            ],
            axis=1,
        )
        own_preact = own_rows(grad_preact).astype(BF16)
        grad_preact = grad_preact.astype(BF16)
        for tap in range(2):
            tap_grad = mm(taps_t[layer, tap], own_preact)
            for ref, half in places:
                for y_low in range(2):
                    top = half * 128 + y_low * 64
                    for x in range(4):
                        columns = slice(x * 128, (x + 1) * 128)
                        for low in range(2):
                            base = 256 + low * 384 + layer * 128
                            ref[tap * 2 + y_low, x, :, base : base + 128] = tap_grad[
                                top + low * 32 : top + low * 32 + 32, columns
                            ].astype(BF16)
        grad_joined = mm_nt(grad_preact, w_f[layer]).astype(BF16)
        past = grad_joined[:, :NODES].astype(F32)
        now = grad_joined[:, NODES:].astype(F32)
        earlier = pltpu.roll(past, ALL_ROWS - 2**layer, 0)
        grad = ((grad_wide + now).astype(BF16).astype(F32) + earlier).astype(BF16)
    own = own_rows(grad.astype(F32)).astype(BF16)
    store_small(3, mm(cov_t[...], own))
    result = mm_nt(own, w_in[...]).astype(BF16)
    for b in range(SEQ):
        cov_grad[b] = result[b * ROWS : (b + 1) * ROWS]


def add_kernel(keep, got, out):
    out[...] = keep[...] + got[...]


def join_kernel(score, keep, got, out):
    out[:, :, :, :1024] = score[...]
    out[:, :, :, 1024:] = keep[...] + got[...]


def plane_kernel(pieces, out):
    total = pieces[0].astype(F32)
    for i in range(1, pieces.shape[0]):
        total = total + pieces[i].astype(F32)
    for z in range(8):
        r = slice(z * 4, z * 4 + 4)
        first = jnp.concatenate([total[r, :512], total[r, 1024:1152]], axis=1)
        second = jnp.concatenate([total[r, 512:1024], total[r, 1152:1280]], axis=1)
        low = z % 4
        base = 1280 + (z // 4) * 384
        taps = total[low * 8 : low * 8 + 8, base : base + 384]
        both = jnp.concatenate([first, second], axis=0)
        out[z] = jnp.concatenate([both, taps], axis=1).astype(BF16)


def line_kernel(pieces, out):
    total = pieces[0].astype(F32)
    for i in range(1, pieces.shape[0]):
        total = total + pieces[i].astype(F32)
    for x in range(out.shape[0]):
        out[x] = total.astype(BF16)


def finish_kernel(g, input_grad, filter_grad, mixing_grad, output_grad):
    for x in range(4):
        v = g[x].astype(F32)
        output_grad[:, x * 1024 : x * 1024 + 512] = v[:4, :512].astype(BF16)
        output_grad[:, x * 1024 + 512 : (x + 1) * 1024] = v[4:, :512].astype(BF16)
        small = jnp.concatenate([v[:4, 512:640], v[4:, 512:640]], axis=1).astype(BF16)
        if x < LAYERS:
            mixing_grad[x] = small
        else:
            input_grad[...] = small
        for layer in range(LAYERS):
            base = 640 + layer * 128
            filter_grad[layer, :, x * 128 : (x + 1) * 128] = v[:, base : base + 128].astype(BF16)


HBM = pl.BlockSpec(memory_space=pltpu.HBM)
ANY = pl.BlockSpec(memory_space=pl.ANY)
WHOLE = pl.BlockSpec(memory_space=VMEM)


def call(kernel, out_shape, in_specs, scratch=(), limit=16, name=None, cost=None):
    return pl.pallas_call(
        kernel,
        out_shape=out_shape,
        in_specs=in_specs,
        out_specs=jax.tree.map(lambda _: WHOLE, out_shape),
        scratch_shapes=scratch,
        compiler_params=pltpu.CompilerParams(vmem_limit_bytes=limit * 1024 * 1024),
        name=name,
        cost_estimate=cost,
    )


def per_device(cov, obs, w_in, w_f, w_m, w_out):
    count = lax.axis_size(TM)
    cov, obs, w_in, w_f, w_m, w_out = (
        pltpu.with_memory_space_constraint(a, pltpu.HBM) for a in (cov, obs, w_in, w_f, w_m, w_out)
    )
    edge = shape((SEQ, HALO, 2 * NODES), F32)
    to_pair, to_far, squares = call(
        start_kernel,
        (edge, edge, shape((count, SEQ, 128), F32)),
        [HBM, HBM],
        scratch=[
            VMEM((SEQ, 16, NODES), BF16),
            VMEM((SEQ, 16, NODES), BF16),
            VMEM(obs.shape, F32),
            pltpu.SemaphoreType.DMA((3,)),
        ],
        limit=4,
        name="start",
    )(cov, obs)
    sums = lax.all_to_all(squares, TM, 0, 0, tiled=True)
    from_pair = lax.ppermute(to_pair, "core", [(0, 1), (1, 0)])
    seams = [(i, i + 1) for i in range(1, count - 1, 2)]
    from_far = lax.ppermute(to_far, TM, seams + [(j, i) for i, j in seams])

    part = shape((4, 4, 32, 1024), BF16)
    act = shape((LAYERS, ALL_ROWS, NODES), F32)
    grad, send_score, keep_score, *saved = call(
        score_kernel,
        (
            shape((ALL_ROWS, NODES), BF16),
            part,
            part,
            act,
            act,
            shape((NODES, OWN), BF16),
            shape((LAYERS, NODES, OWN), BF16),
            shape((LAYERS, 2, NODES, OWN), BF16),
            shape(w_in.shape, BF16),
            shape(w_f.shape, BF16),
            shape(w_m.shape, BF16),
        ),
        [WHOLE, WHOLE, WHOLE] + [HBM] * 6,
        scratch=[
            VMEM((ALL_HEAD, SCENARIOS * NODES), F32),
            VMEM((ALL_HEAD, NODES), F32),
            VMEM(cov.shape, BF16),
            VMEM(obs.shape, F32),
            VMEM(w_out.shape, BF16),
            VMEM((ALL_HEAD, SCENARIOS * NODES), BF16),
            VMEM((NODES, OWN), BF16),
            pltpu.SemaphoreType.DMA((6,)),
        ],
        limit=36,
        name="score",
        cost=pl.CostEstimate(flops=10**10, transcendentals=0, bytes_accessed=10**7),
    )(from_pair, from_far, sums, cov, obs, w_in, w_f, w_m, w_out)
    swap = [(0, 1), (1, 0)]
    got_score = lax.ppermute(send_score, "core", swap)
    cov_grad, send_rest, keep_rest = call(
        layers_kernel,
        (shape((SEQ, ROWS, NODES), BF16), part, part),
        [WHOLE] * 9,
        limit=16,
        name="layers",
        cost=pl.CostEstimate(flops=4 * 10**9, transcendentals=0, bytes_accessed=10**7),
    )(grad, *saved)
    got_rest = lax.ppermute(send_rest, "core", swap)
    score = call(add_kernel, part, [WHOLE] * 2, limit=4, name="pair")(keep_score, got_score)
    chip = call(join_kernel, shape((4, 4, 32, 2048), BF16), [WHOLE] * 3, limit=4, name="join")(
        score, keep_rest, got_rest
    )
    plane = lax.all_to_all(chip.reshape(16, 32, 2048), ("y", "x"), 0, 0, tiled=True)
    by_z = call(plane_kernel, shape((8, 8, 1024), BF16), [WHOLE], limit=4, name="plane")(plane)
    line = lax.all_to_all(by_z, "z", 0, 0, tiled=True)
    mine = call(line_kernel, shape((4, 8, 1024), BF16), [WHOLE], limit=4, name="line")(line)
    whole = lax.all_to_all(mine, "x", 0, 0, tiled=True)
    input_grad, filter_grad, mixing_grad, output_grad = call(
        finish_kernel,
        (
            shape((4, NODES), BF16),
            shape((LAYERS, 8, 2 * NODES), BF16),
            shape((LAYERS, 4, NODES), BF16),
            shape((4, SCENARIOS * NODES), BF16),
        ),
        [WHOLE],
        limit=4,
        name="finish",
    )(whole)
    return (cov_grad, input_grad, filter_grad, mixing_grad, output_grad)


def solution(mesh):
    inner = Mesh(mesh.devices.reshape(4, 8, 2, 4), ("y", "z", "core", "x"))
    data = P("x", TM, None)
    return jax.shard_map(
        per_device,
        mesh=inner,
        in_specs=(data, data, P(), P(), P(), P()),
        out_specs=(data, P(TM, None), P(None, TM, None), P(None, TM, None), P(TM, None)),
        check_vma=False,
    )
```
